32 devices in a mesh: groups: 2 (over y), blk: 4 (over z), rep: 4 (over x, core).
Axes of the slice: x: 2, y: 2, z: 4, core: 2. Of those that a mesh axis runs over, the one named last changes fastest.
Arguments:
- orbitals: float32 [8, 262144], P(('groups', 'blk')), parts along dimension 0, may hold values from -6 to 6
- offsets: int32 [8], P('groups'), parts along dimension 0, may hold values from 0 to 3
Outputs:
- exchanged: float32 [8, 262144], P(('groups', 'blk'), 'rep'), parts along dimension 0
- margin: float32 [8, 4], P(('groups', 'blk')), parts along dimension 0
The draws below stay inside these ranges and needn't reach their ends.
There are 2 independent parts, one for each index of `groups`. The reference program is written for one: setup_inputs(seed, part) draws one part's arguments, and reference() takes and returns one part's arrays. A program takes and returns all parts, laid end to end along the dimension named above; each array names one. Nothing has to cross between parts.
All inputs are finite; a program needn't handle non-finite values.
Results may differ from the reference program's by a relative error of at most 0.0001.
Values sent between devices are 32-bit elements; how exact they have to be, the bound alone decides.
No kernel may reach another device: no remote copies, remote signals or barrier semaphores. Data moves between devices by JAX's collectives and lax.ppermute only.
A program may use at most 64 MiB of HBM per device.

```python
import jax
import jax.numpy as jnp
from jax import lax

NG = 64
OB = 1
STEPS = 3
NORB = 4
CELLS = 262144
N_BLK = 4
N_REP = 4


def set_ends(drawn, stream_key, smallest, top_value):
    index_at = [jax.random.randint(jax.random.fold_in(stream_key, axis), (), 0, length) for axis, length in enumerate(drawn.shape)]
    widest = drawn.shape.index(max(drawn.shape))
    beside = index_at[:widest] + [(index_at[widest] + 1) % drawn.shape[widest]] + index_at[widest + 1:]
    return drawn.at[tuple(index_at)].set(smallest).at[tuple(beside)].set(top_value)


def level_of(own_key, shape, shards, low, high):
    loudness = 1.0
    for axis_at, parts in shards:
        heights = jax.random.uniform(jax.random.fold_in(jax.random.fold_in(own_key, 6), axis_at), (parts,), jnp.float32, low / len(shards), high / len(shards))
        loudness = loudness * jnp.repeat(jnp.exp(heights), shape[axis_at] // parts).reshape((-1,) + (1,) * (len(shape) - 1 - axis_at))
    return loudness


def centred(stream_key, shape, deviation, reach, split=(), held_as=jnp.bfloat16):
    array = jax.random.normal(stream_key, shape, jnp.float32) * deviation
    if len(split) > 0:
        array = level_of(stream_key, shape, split, -0.22, 0.18) * array
    return jnp.clip(array, min=-reach, max=reach).astype(held_as)


def setup_inputs(seed: int = 0, part: int = 0) -> dict:
    splits = jax.random.split(jax.random.key(seed), 3)
    part_keys = jax.random.split(jax.random.fold_in(splits[2], part), 3)
    orbitals = centred(part_keys[0], (NORB, CELLS), 1.0, 6.0, ((0, 4),), jnp.float32)
    offsets = set_ends(jax.random.randint(part_keys[1], (N_REP,), 0, N_BLK), jax.random.fold_in(part_keys[1], 1), 0, N_BLK - 1).astype(jnp.int32)
    return {"orbitals": orbitals, "offsets": offsets}


precise_mode = lax.Precision.HIGHEST
screen_scale = 0.05


def cas_table(grid_points):
    grid_index = jnp.arange(grid_points, dtype=jnp.int32)
    product = (grid_index[:, None] * grid_index[None, :]) % grid_points
    phase_angle = (2.0 * jnp.pi / grid_points) * product.astype(jnp.float32)
    return jnp.cos(phase_angle) + jnp.sin(phase_angle)


def screened_kernel(grid_points):
    grid_index = jnp.arange(grid_points, dtype=jnp.int32)
    folded = jnp.where(grid_index <= grid_points // 2, grid_index, grid_index - grid_points).astype(jnp.float32)
    squares = folded * folded
    k_squared = squares[:, None, None] + squares[None, :, None] + squares[None, None, :]
    safe_square = jnp.maximum(k_squared, 1.0)
    screened = (4.0 * jnp.pi / (screen_scale * safe_square)) * (1.0 - jnp.exp(-screen_scale * safe_square / (4.0 * jnp.pi)))
    return jnp.where(k_squared > 0.5, screened, jnp.ones_like(screened))


def hartley_cube(values_field, cas_values):
    values_field = jnp.einsum('kx,abxyz->abkyz', cas_values, values_field, precision=precise_mode)
    values_field = jnp.einsum('ky,abxyz->abxkz', cas_values, values_field, precision=precise_mode)
    return jnp.einsum('kz,abxyz->abxyk', cas_values, values_field, precision=precise_mode)


def reference(orbitals, offsets):
    cas_values = cas_table(NG)
    kernel = screened_kernel(NG)
    blocks_all = orbitals.reshape(N_BLK, OB, NG, NG, NG)
    cycle_index = jnp.arange(N_BLK, dtype=jnp.int32)
    accumulator = jnp.zeros_like(blocks_all)

    def one_block(pair_items):
        own_block, vis_block = pair_items
        density = own_block[:, None] * vis_block[None, :]
        potential = hartley_cube(hartley_cube(density, cas_values) * kernel, cas_values) / float(NG ** 3)
        return jnp.sum(potential * vis_block[None, :], axis=1)

    for replica in range(N_REP):
        for step_index in range(STEPS):
            source_block = (cycle_index - offsets[replica] - step_index) % N_BLK
            visiting = jnp.take(blocks_all, source_block.astype(jnp.int32), axis=0)
            accumulator = accumulator + lax.map(one_block, (blocks_all, visiting))
    exchanged = accumulator.reshape(NORB, NG ** 3)
    margin = lax.dot_general(orbitals, exchanged, (((1,), (1,)), ((), ())), precision=precise_mode) / float(NG ** 3)
    return exchanged, margin
```

```python
import functools

import jax
import jax.numpy as jnp
from jax import lax
from jax.experimental import pallas as pl
from jax.experimental.pallas import tpu as pltpu
from jax.sharding import PartitionSpec as P

NG = 64
STEPS = 3
LANES = 128
HALF = LANES // 2
screen_scale = 0.05


def passed_along(block, axis, distance):
    devices = range(lax.axis_size(axis))
    route = [((i - distance) % len(devices), i) for i in devices]
    return lax.ppermute(block, axis, route)


def cas_table(grid_points):
    grid_index = jnp.arange(grid_points, dtype=jnp.int32)
    product = grid_index[:, None] * grid_index[None, :] % grid_points
    phase_angle = 2.0 * jnp.pi / grid_points * product.astype(jnp.float32)
    return jnp.cos(phase_angle) + jnp.sin(phase_angle)


def screened_kernel(grid_points):
    def squares(index):
        folded = jnp.where(index <= grid_points // 2, index, index - grid_points).astype(jnp.float32)
        return folded * folded

    shape = (grid_points * grid_points // 2, 2 * grid_points)
    row = lax.broadcasted_iota(jnp.int32, shape, 0)
    lane = lax.broadcasted_iota(jnp.int32, shape, 1)
    k_squared = (
        squares(row % grid_points)
        + squares(2 * (row // grid_points) + lane // grid_points)
        + squares(lane % grid_points)
    )
    safe_square = jnp.maximum(k_squared, 1.0)
    screened = (
        4.0
        * jnp.pi
        / (screen_scale * safe_square)
        * (1.0 - jnp.exp(-screen_scale * safe_square / (4.0 * jnp.pi)))
    )
    return jnp.where(k_squared > 0.5, screened, jnp.ones_like(screened))


def high_low(value):
    high = value.astype(jnp.bfloat16)
    return high, (value - high.astype(jnp.float32)).astype(jnp.bfloat16)


def dot(a, b):
    return lax.dot_general(a, b, (((1,), (0,)), ((), ())), preferred_element_type=jnp.float32)


def swapped(first, second, low_half):
    return (
        jnp.where(low_half, first, pltpu.roll(second, HALF, 1)),
        jnp.where(low_half, pltpu.roll(first, HALF, 1), second),
    )


def left_weights(table):
    high, low = high_low(table)
    return jnp.concatenate([high, high, low], axis=1)


def lane_weights(table):
    high, low = high_low(table)
    return jnp.concatenate(
        [jnp.concatenate([high, low], axis=1), jnp.concatenate([high, jnp.zeros_like(low)], axis=1)],
        axis=0,
    )


def from_left(weights, value):
    high, low = high_low(value)
    return dot(weights, jnp.concatenate([high, low, high], axis=0))


def along_lanes(value, weights):
    high, low = high_low(value)
    both = dot(jnp.concatenate([high, low], axis=1), weights)
    return both[:, :LANES] + both[:, LANES:]


def low_mask(rows):
    return lax.broadcasted_iota(jnp.int32, (rows, LANES), 1) < HALF


def spectrum_body(own, visiting, kernel, forward, backward, paired, out):
    plane = NG // 2
    pairs = NG // 2
    mask = low_mask(plane)
    w_forward = left_weights(forward[...])
    w_backward = left_weights(backward[...])
    w_lanes = lane_weights(paired[...])

    def planes(step, _):
        at = pl.multiple_of(step * (4 * plane), 4 * plane)
        density = own[pl.ds(at, 4 * plane), :] * visiting[pl.ds(at, 4 * plane), :]
        along_z = along_lanes(density, w_lanes)
        blocks = []
        for half in range(2):
            base = half * 2 * plane
            even, odd = swapped(along_z[base : base + plane], along_z[base + plane : base + 2 * plane], mask)
            blocks.append(jnp.concatenate([even, odd], axis=0))
        along_y = from_left(w_forward, jnp.concatenate(blocks, axis=1))
        out[pl.ds(at, 2 * plane), :] = along_y[:, :LANES]
        out[pl.ds(at + 2 * plane, 2 * plane), :] = along_y[:, LANES:]
        return 0

    lax.fori_loop(0, NG // 4, planes, 0, unroll=2)

    def columns(step, _):
        blocks = []
        for part in range(2):
            row = 4 * step + 2 * part
            first = out[pl.ds(row, pairs, stride=NG), :]
            second = out[pl.ds(row + 1, pairs, stride=NG), :]
            blocks.append(jnp.concatenate(swapped(first, second, mask), axis=0))
        along_x = from_left(w_forward, jnp.concatenate(blocks, axis=1))
        at = pl.multiple_of(step * (2 * NG), 2 * NG)
        weight = jnp.concatenate([kernel[pl.ds(at, NG), :], kernel[pl.ds(at + NG, NG), :]], axis=1)
        returned = from_left(w_backward, along_x * weight)
        for part in range(2):
            block = returned[:, part * LANES : (part + 1) * LANES]
            first, second = swapped(block[:plane], block[plane:], mask)
            row = 4 * step + 2 * part
            out[pl.ds(row, pairs, stride=NG), :] = first
            out[pl.ds(row + 1, pairs, stride=NG), :] = second
        return 0

    lax.fori_loop(0, NG // 4, columns, 0, unroll=2)


def spectrum(own, visiting, kernel, forward, backward, paired):
    rows = own.shape[0]
    return pl.pallas_call(
        spectrum_body,
        out_shape=jax.ShapeDtypeStruct((rows, LANES), jnp.float32),
        in_specs=[pl.BlockSpec(memory_space=pltpu.VMEM)] * 6,
        out_specs=pl.BlockSpec(memory_space=pltpu.VMEM),
        compiler_params=pltpu.CompilerParams(vmem_limit_bytes=24 << 20),
        cost_estimate=pl.CostEstimate(flops=rows * LANES * NG * 24, bytes_accessed=16 * rows * LANES, transcendentals=0),
        name="spectrum",
    )(own, visiting, kernel, forward, backward, paired)


def term_body(chosen, spectral, visiting, scale, backward, paired, out):
    plane = NG // 2
    mask = low_mask(plane)
    w_backward = left_weights(backward[...])
    w_lanes = lane_weights(paired[...])
    factor = scale[0]

    def planes(step, _):
        at = pl.multiple_of(step * (4 * plane), 4 * plane)
        pair = jnp.concatenate(
            [spectral[pl.ds(at, 2 * plane), :], spectral[pl.ds(at + 2 * plane, 2 * plane), :]], axis=1
        )
        along_y = from_left(w_backward, pair)
        blocks = []
        for half in range(2):
            block = along_y[:, half * LANES : (half + 1) * LANES]
            blocks.extend(swapped(block[:plane], block[plane:], mask))
        potential = along_lanes(jnp.concatenate(blocks, axis=0), w_lanes)
        out[pl.ds(at, 4 * plane), :] = potential * (visiting[pl.ds(at, 4 * plane), :] * factor)
        return 0

    lax.fori_loop(0, spectral.shape[0] // (4 * plane), planes, 0, unroll=2)


def term(slabs, slab_rows, spectral, visiting, scale, backward, paired):
    count = slabs.shape[0]
    slab = pl.BlockSpec((slab_rows, LANES), lambda i, chosen: (chosen[i], 0))
    whole = pl.BlockSpec(memory_space=pltpu.VMEM)
    cells = count * slab_rows * LANES
    return pl.pallas_call(
        term_body,
        out_shape=jax.ShapeDtypeStruct((count * slab_rows, LANES), jnp.float32),
        grid_spec=pltpu.PrefetchScalarGridSpec(
            num_scalar_prefetch=1,
            grid=(count,),
            in_specs=[slab, slab, pl.BlockSpec(memory_space=pltpu.SMEM), whole, whole],
            out_specs=pl.BlockSpec((slab_rows, LANES), lambda i, chosen: (i, 0)),
        ),
        compiler_params=pltpu.CompilerParams(vmem_limit_bytes=24 << 20),
        cost_estimate=pl.CostEstimate(flops=cells * NG * 12, bytes_accessed=12 * cells, transcendentals=0),
        name="term",
    )(slabs, spectral, visiting, scale, backward, paired)


def position_block(orbital_block, amount):
    bit_count = (lax.axis_size("blk") - 1).bit_length()
    for bit_level in range(bit_count):
        moved_block = passed_along(orbital_block, "blk", 1 << bit_level)
        orbital_block = jnp.where(amount // (1 << bit_level) % 2 == 1, moved_block, orbital_block)
    return orbital_block


def displacement_order(blocks):
    order = []
    for distance in range(1, blocks // 2 + 1):
        order += [distance] if 2 * distance == blocks else [distance, blocks - distance]
    return order + [0]


def shared_visits(orbitals, offsets, replica):
    blocks, replicas = lax.axis_size("blk"), lax.axis_size("rep")
    order = displacement_order(blocks)
    met = (offsets[:, None] + jnp.arange(STEPS, dtype=jnp.int32)[None, :]) % blocks
    visits = []
    for slot in range(blocks // replicas):
        chosen = order[slot * replicas : (slot + 1) * replicas]
        route = [
            ((b - chosen[r]) % blocks * replicas + r, b * replicas + r)
            for b in range(blocks)
            for r in range(replicas)
            if chosen[r] != 0
        ]
        displacement = jnp.asarray(chosen, jnp.int32)[replica]
        moved = lax.ppermute(orbitals, ("blk", "rep"), route)
        if 0 in chosen:
            moved = jnp.where(displacement == 0, orbitals, moved)
        weight = jnp.sum((met == displacement).astype(jnp.float32))
        visits.append((moved, weight))
    return visits


def stepped_visits(orbitals, offsets, replica):
    blocks = lax.axis_size("blk")
    first = position_block(orbitals, (offsets[replica] + STEPS // 2) % blocks)
    visits = [first]
    for distance in range(1, STEPS // 2 + 1):
        visits.append(passed_along(first, "blk", -distance))
        visits.append(passed_along(first, "blk", distance))
    return [(visit, jnp.ones((), jnp.float32)) for visit in visits]


def local(orbitals, offsets):
    blocks, replicas = lax.axis_size("blk"), lax.axis_size("rep")
    replica = lax.axis_index("rep")
    cells = orbitals.shape[1]
    rows = cells // LANES
    slab_rows = rows // replicas
    table = cas_table(NG)
    forward = table.reshape(NG, NG // 2, 2).transpose(0, 2, 1).reshape(NG, NG)
    backward = forward.T
    paired = jnp.kron(jnp.eye(2, dtype=jnp.float32), table)
    kernel = screened_kernel(NG)
    own = orbitals.reshape(rows, LANES)

    if blocks % replicas == 0 and blocks // replicas < STEPS:
        visits = shared_visits(orbitals, offsets, replica)
    else:
        visits = stepped_visits(orbitals, offsets, replica)

    quarter = lax.dynamic_slice_in_dim(orbitals, replica * (cells // replicas), cells // replicas, 1)
    slab_orbitals = lax.all_to_all(quarter, "blk", split_axis=1, concat_axis=0, tiled=True)

    terms = []
    for visit, weight in visits:
        visiting = visit.reshape(rows, LANES)
        spectral = spectrum(own, visiting, kernel, forward, backward, paired)
        terms.append((spectral, visiting, (weight / float(NG**3)).reshape(1)))

    def summed(slabs):
        total = None
        for spectral, visiting, scale in terms:
            part = term(slabs, slab_rows, spectral, visiting, scale, backward, paired)
            total = part if total is None else total + part
        return total

    if replicas == 4:
        low, high = replica % 2, replica // 2
        sent = summed(jnp.stack([1 - low, 3 - low]))
        kept_far = summed((2 * (1 - high) + low).reshape(1))
        kept = summed((2 * high + low).reshape(1))
        met = lax.ppermute(sent, "rep", [(r, r ^ 1) for r in range(replicas)]).reshape(2, slab_rows, LANES)
        far = kept_far + jnp.where(high == 0, met[1], met[0])
        near = kept + jnp.where(high == 0, met[0], met[1])
        exchanged = near + lax.ppermute(far, "rep", [(r, r ^ 2) for r in range(replicas)])
        exchanged = exchanged.reshape(1, cells // replicas)
    else:
        whole = summed(jnp.arange(replicas, dtype=jnp.int32)).reshape(1, cells)
        exchanged = lax.psum_scatter(whole, "rep", scatter_dimension=1, tiled=True)

    slab_exchanged = lax.all_to_all(exchanged, "blk", split_axis=1, concat_axis=0, tiled=True)
    partial_value = jnp.sum(slab_orbitals[:, None, :] * slab_exchanged[None, :, :], axis=2) / float(NG**3)
    gram_rows = lax.psum_scatter(partial_value, "blk", scatter_dimension=0, tiled=True)
    margin = lax.psum(gram_rows, "rep")
    return (exchanged, margin)


def solution(mesh):
    placed = (P(("groups", "blk"), None), P("groups"))
    return jax.shard_map(
        local,
        mesh=mesh,
        in_specs=placed,
        out_specs=(P(("groups", "blk"), "rep"), P(("groups", "blk"), None)),
        check_vma=False,
    )
```

```python
import functools

import jax
import jax.numpy as jnp
from jax import lax
from jax.experimental import pallas as pl
from jax.experimental.pallas import tpu as pltpu
from jax.sharding import PartitionSpec as P

NG = 64
STEPS = 3
LANES = 128
HALF = LANES // 2
PITCH = NG + 1
MET = (3, 1, 2, 0)
SENT = (3, 1, 2, 1)
screen_scale = 0.05


def passed_along(block, axis, distance):
    devices = range(lax.axis_size(axis))
    route = [((i - distance) % len(devices), i) for i in devices]
    return lax.ppermute(block, axis, route)


def cas_table(grid_points):
    grid_index = jnp.arange(grid_points, dtype=jnp.int32)
    product = grid_index[:, None] * grid_index[None, :] % grid_points
    phase_angle = 2.0 * jnp.pi / grid_points * product.astype(jnp.float32)
    return jnp.cos(phase_angle) + jnp.sin(phase_angle)


def screened_kernel(grid_points):
    def squares(index):
        folded = jnp.where(index <= grid_points // 2, index, index - grid_points).astype(jnp.float32)
        return folded * folded

    shape = (grid_points * grid_points // 2, 2 * grid_points)
    row = lax.broadcasted_iota(jnp.int32, shape, 0)
    lane = lax.broadcasted_iota(jnp.int32, shape, 1)
    k_squared = (
        squares(row % grid_points)
        + squares(2 * (row // grid_points) + lane // grid_points)
        + squares(lane % grid_points)
    )
    safe_square = jnp.maximum(k_squared, 1.0)
    screened = (
        4.0
        * jnp.pi
        / (screen_scale * safe_square)
        * (1.0 - jnp.exp(-screen_scale * safe_square / (4.0 * jnp.pi)))
    )
    return jnp.where(k_squared > 0.5, screened, jnp.ones_like(screened))


def high_low(value):
    high = value.astype(jnp.bfloat16)
    return high, (value - high.astype(jnp.float32)).astype(jnp.bfloat16)


def dot(a, b):
    return lax.dot_general(a, b, (((1,), (0,)), ((), ())), preferred_element_type=jnp.float32)


def swapped(first, second, low_half):
    return (
        jnp.where(low_half, first, pltpu.roll(second, HALF, 1)),
        jnp.where(low_half, pltpu.roll(first, HALF, 1), second),
    )


def left_weights(table):
    high, low = high_low(table)
    return jnp.concatenate([high, high, low], axis=1)


def lane_weights(table):
    high, low = high_low(table)
    return jnp.concatenate(
        [jnp.concatenate([high, low], axis=1), jnp.concatenate([high, jnp.zeros_like(low)], axis=1)],
        axis=0,
    )


def from_left(weights, value):
    high, low = high_low(value)
    return dot(weights, jnp.concatenate([high, low, high], axis=0))


def along_lanes(value, weights):
    high, low = high_low(value)
    both = dot(jnp.concatenate([high, low], axis=1), weights)
    return both[:, :LANES] + both[:, LANES:]


def low_mask(rows):
    return lax.broadcasted_iota(jnp.int32, (rows, LANES), 1) < HALF


def spectrum_body(same, own, *refs):
    *pieces, kernel, forward, backward, paired, out = refs
    alone = same[0] == 1
    plane = NG // 2
    pairs = NG // 2
    mask = low_mask(plane)
    w_forward = left_weights(forward[...])
    w_backward = left_weights(backward[...])
    w_lanes = lane_weights(paired[...])

    def planes(piece, first_row, step, _):
        at = pl.multiple_of(step * (4 * plane), 4 * plane)
        mine = own[pl.ds(at, 4 * plane), :]
        density = mine * jnp.where(alone, mine, piece[pl.ds(at - first_row, 4 * plane), :])
        along_z = along_lanes(density, w_lanes)
        blocks = []
        for half in range(2):
            base = half * 2 * plane
            even, odd = swapped(along_z[base : base + plane], along_z[base + plane : base + 2 * plane], mask)
            blocks.append(jnp.concatenate([even, odd], axis=0))
        along_y = from_left(w_forward, jnp.concatenate(blocks, axis=1))
        out[pl.ds(step * (2 * PITCH), NG), :] = along_y[:, :LANES]
        out[pl.ds(step * (2 * PITCH) + PITCH, NG), :] = along_y[:, LANES:]
        return 0

    each = NG // 4 // len(pieces)
    for index, piece in enumerate(pieces):
        first_row = index * each * 4 * plane
        lax.fori_loop(
            index * each, (index + 1) * each, functools.partial(planes, piece, first_row), 0, unroll=each
        )

    def columns(step, _):
        blocks = []
        for part in range(2):
            row = 4 * step + 2 * part
            first = out[pl.ds(row, pairs, stride=PITCH), :]
            second = out[pl.ds(row + 1, pairs, stride=PITCH), :]
            blocks.append(jnp.concatenate(swapped(first, second, mask), axis=0))
        along_x = from_left(w_forward, jnp.concatenate(blocks, axis=1))
        at = pl.multiple_of(step * (2 * NG), 2 * NG)
        weight = jnp.concatenate([kernel[pl.ds(at, NG), :], kernel[pl.ds(at + NG, NG), :]], axis=1)
        returned = from_left(w_backward, along_x * weight)
        for part in range(2):
            block = returned[:, part * LANES : (part + 1) * LANES]
            first, second = swapped(block[:plane], block[plane:], mask)
            row = 4 * step + 2 * part
            out[pl.ds(row, pairs, stride=PITCH), :] = first
            out[pl.ds(row + 1, pairs, stride=PITCH), :] = second
        return 0

    lax.fori_loop(0, NG // 4, columns, 0, unroll=16)


def spectrum(same, own, pieces, kernel, forward, backward, paired):
    rows = own.shape[0]
    vmem = pl.BlockSpec(memory_space=pltpu.VMEM)
    return pl.pallas_call(
        spectrum_body,
        out_shape=jax.ShapeDtypeStruct((NG // 2 * PITCH, LANES), jnp.float32),
        in_specs=[pl.BlockSpec(memory_space=pltpu.SMEM)] + [vmem] * (5 + len(pieces)),
        out_specs=vmem,
        compiler_params=pltpu.CompilerParams(vmem_limit_bytes=24 << 20),
        cost_estimate=pl.CostEstimate(
            flops=rows * LANES * NG * 24, bytes_accessed=16 * rows * LANES, transcendentals=0
        ),
        name="spectrum",
    )(same, own, *pieces, kernel, forward, backward, paired)


def term_body(chosen, same, spectral, own, *refs):
    *pieces, backward, paired, out = refs
    plane = NG // 2
    mask = low_mask(plane)
    w_backward = left_weights(backward[...])
    w_lanes = lane_weights(paired[...])
    slab_rows = out.shape[0]
    slab = chosen[pl.program_id(0)]
    each = own.shape[0] // len(pieces)
    alone = same[0] == 1

    def partner(at):
        row = pl.multiple_of(slab * slab_rows, slab_rows) + at
        value = pieces[0][pl.ds(row % each, 4 * plane), :]
        for index in range(1, len(pieces)):
            value = jnp.where(row // each == index, pieces[index][pl.ds(row % each, 4 * plane), :], value)
        return jnp.where(alone, own[pl.ds(row, 4 * plane), :], value)

    def planes(step, _):
        at = pl.multiple_of(step * (4 * plane), 4 * plane)
        row = step * (2 * PITCH)
        pair = jnp.concatenate([spectral[pl.ds(row, NG), :], spectral[pl.ds(row + PITCH, NG), :]], axis=1)
        along_y = from_left(w_backward, pair)
        blocks = []
        for half in range(2):
            block = along_y[:, half * LANES : (half + 1) * LANES]
            blocks.extend(swapped(block[:plane], block[plane:], mask))
        potential = along_lanes(jnp.concatenate(blocks, axis=0), w_lanes)
        out[pl.ds(at, 4 * plane), :] = potential * (partner(at) * (1.0 / NG**3))
        return 0

    lax.fori_loop(0, slab_rows // (4 * plane), planes, 0, unroll=4)


def term(slabs, slab_rows, same, spectral, own, pieces, backward, paired):
    count = slabs.shape[0]
    pitched = pl.BlockSpec((slab_rows // NG * PITCH, LANES), lambda i, chosen: (chosen[i], 0))
    whole = pl.BlockSpec(memory_space=pltpu.VMEM)
    cells = count * slab_rows * LANES
    return pl.pallas_call(
        term_body,
        out_shape=jax.ShapeDtypeStruct((count * slab_rows, LANES), jnp.float32),
        grid_spec=pltpu.PrefetchScalarGridSpec(
            num_scalar_prefetch=1,
            grid=(count,),
            in_specs=[pl.BlockSpec(memory_space=pltpu.SMEM), pitched, whole] + [whole] * (2 + len(pieces)),
            out_specs=pl.BlockSpec((slab_rows, LANES), lambda i, chosen: (i, 0)),
        ),
        compiler_params=pltpu.CompilerParams(vmem_limit_bytes=24 << 20),
        cost_estimate=pl.CostEstimate(flops=cells * NG * 12, bytes_accessed=12 * cells, transcendentals=0),
        name="term",
    )(slabs, same, spectral, own, *pieces, backward, paired)


def blend_body(weights, kept, met, *refs, first):
    *more, out = refs
    rows = out.shape[0]
    at = 0 if first else rows
    value = weights[0] * kept[at : at + rows, :] + weights[1] * met[at : at + rows, :]
    out[...] = value + more[0][...] if more else value


def blend(weights, kept, met, *more):
    rows = kept.shape[0] // 2
    vmem = pl.BlockSpec(memory_space=pltpu.VMEM)
    return pl.pallas_call(
        functools.partial(blend_body, first=not more),
        out_shape=jax.ShapeDtypeStruct((rows, LANES), jnp.float32),
        in_specs=[pl.BlockSpec(memory_space=pltpu.SMEM)] + [vmem] * (2 + len(more)),
        out_specs=vmem,
        compiler_params=pltpu.CompilerParams(vmem_limit_bytes=16 << 20),
        cost_estimate=pl.CostEstimate(flops=4 * rows * LANES, bytes_accessed=16 * rows * LANES, transcendentals=0),
        name="blend",
    )(weights, kept, met, *more)


def gram_body(places, factors, kept, met, own, *refs):
    *stores, out = refs
    visits, nears, evens, odds = stores[0:2], stores[2:4], stores[4:6], stores[6:8]
    slab_rows = kept.shape[0] // 2
    chunk = 64
    parity = places[6]

    def folded(value):
        return jnp.sum(value.reshape(chunk // 8, 8, LANES), axis=0)

    totals = (jnp.zeros((8, LANES), jnp.float32),) * 8
    for side in range(2):
        term_row = pl.multiple_of(places[4 + side], slab_rows)
        half_row = pl.multiple_of(parity * slab_rows, slab_rows)

        def step(index, totals, side=side, term_row=term_row, half_row=half_row):
            at = pl.multiple_of(index * chunk, chunk)
            terms = (kept[pl.ds(term_row + at, chunk), :], met[pl.ds(term_row + at, chunk), :])
            orbitals = (
                own[pl.ds(side * 2 * slab_rows + half_row + at, chunk), :],
                visits[side][pl.ds(half_row + at, chunk), :],
                nears[side][pl.ds(half_row + at, chunk), :],
                evens[side][pl.ds(at, chunk), :] + odds[side][pl.ds(at, chunk), :],
            )
            return tuple(
                totals[4 * t + o] + folded(terms[t] * orbitals[o]) for t in range(2) for o in range(4)
            )

        totals = lax.fori_loop(0, slab_rows // chunk, step, totals, unroll=2)
    lane = lax.broadcasted_iota(jnp.int32, (8, LANES), 1)
    result = jnp.zeros((8, LANES), jnp.float32)
    for o in range(4):
        value = jnp.sum(factors[o] * totals[o] + factors[4 + o] * totals[4 + o], axis=(0, 1), keepdims=True)
        result = jnp.where(lane == places[o], value, result)
    out[...] = result


def gram(places, factors, kept, met, own, *stores):
    rows = kept.shape[0]
    smem = pl.BlockSpec(memory_space=pltpu.SMEM)
    vmem = pl.BlockSpec(memory_space=pltpu.VMEM)
    return pl.pallas_call(
        gram_body,
        out_shape=jax.ShapeDtypeStruct((8, LANES), jnp.float32),
        in_specs=[smem, smem] + [vmem] * (3 + len(stores)),
        out_specs=vmem,
        compiler_params=pltpu.CompilerParams(vmem_limit_bytes=24 << 20),
        cost_estimate=pl.CostEstimate(flops=16 * rows * LANES, bytes_accessed=24 * rows * LANES, transcendentals=0),
        name="gram",
    )(places, factors, kept, met, own, *stores)


def position_block(orbital_block, amount):
    bit_count = (lax.axis_size("blk") - 1).bit_length()
    for bit_level in range(bit_count):
        moved_block = passed_along(orbital_block, "blk", 1 << bit_level)
        orbital_block = jnp.where(amount // (1 << bit_level) % 2 == 1, moved_block, orbital_block)
    return orbital_block


def stepped(orbitals, offsets, tables):
    blocks, replicas = lax.axis_size("blk"), lax.axis_size("rep")
    replica = lax.axis_index("rep")
    cells = orbitals.shape[1]
    rows = cells // LANES
    kernel, forward, backward, paired = tables
    first = position_block(orbitals, (offsets[replica] + STEPS // 2) % blocks)
    visits = [first]
    for distance in range(1, STEPS // 2 + 1):
        visits.append(passed_along(first, "blk", -distance))
        visits.append(passed_along(first, "blk", distance))
    own = orbitals.reshape(rows, LANES)
    apart = jnp.zeros((1,), jnp.int32)
    slabs = jnp.arange(replicas, dtype=jnp.int32)
    whole = jnp.zeros((rows, LANES), jnp.float32)
    for visit in visits:
        pieces = [visit.reshape(rows, LANES)]
        spectral = spectrum(apart, own, pieces, kernel, forward, backward, paired)
        whole = whole + term(slabs, rows // replicas, apart, spectral, own, pieces, backward, paired)
    exchanged = lax.psum_scatter(whole.reshape(1, cells), "rep", scatter_dimension=1, tiled=True)
    quarter = lax.dynamic_slice_in_dim(orbitals, replica * (cells // replicas), cells // replicas, 1)
    slab_orbitals = lax.all_to_all(quarter, "blk", split_axis=1, concat_axis=0, tiled=True)
    slab_exchanged = lax.all_to_all(exchanged, "blk", split_axis=1, concat_axis=0, tiled=True)
    partial_value = lax.dot_general(
        slab_orbitals, slab_exchanged, (((1,), (1,)), ((), ())), precision=lax.Precision.HIGHEST
    ) / float(NG**3)
    gram_rows = lax.psum_scatter(partial_value, "blk", scatter_dimension=0, tiled=True)
    return exchanged, lax.psum(gram_rows, "rep")


def folded(orbitals, offsets, tables):
    blocks, replicas = lax.axis_size("blk"), lax.axis_size("rep")
    block, replica = lax.axis_index("blk"), lax.axis_index("rep")
    low, high = replica % 2, replica // 2
    cells = orbitals.shape[1]
    rows = cells // LANES
    slab_rows = rows // replicas
    kernel, forward, backward, paired = tables
    own = orbitals.reshape(rows, LANES)
    met_by = jnp.asarray(MET, jnp.int32)
    sent_to = jnp.asarray(SENT, jnp.int32)
    same = (met_by[replica] == 0).astype(jnp.int32).reshape(1)

    def along_blocks(value):
        route = [((b ^ SENT[r]) * replicas + r, b * replicas + r) for b in range(blocks) for r in range(replicas)]
        return lax.ppermute(value, ("blk", "rep"), route)

    def replica_swap(value, bit):
        return lax.ppermute(value, "rep", [(r, r ^ bit) for r in range(replicas)])

    def from_even(value, to_odd):
        return lax.ppermute(value, "rep", [(r, (r ^ 2) + to_odd) for r in range(0, replicas, 2)])

    pieces, nears, evens, odds = [], [], [], []
    for side in range(2):
        piece = along_blocks(own[side * rows // 2 : (side + 1) * rows // 2])
        pieces.append(piece)
    for piece in pieces:
        evens.append(from_even(piece[:slab_rows], 0))
        odds.append(from_even(piece[slab_rows:], 1))
        nears.append(replica_swap(piece, 1))

    spectral = spectrum(same, own, pieces, kernel, forward, backward, paired)
    far_side, near_side = 2 * (1 - high), 2 * high
    sent = term(
        jnp.stack([far_side + 1 - low, near_side + 1 - low]), slab_rows, same, spectral, own, pieces, backward, paired
    )
    kept = term(jnp.stack([far_side + low, near_side + low]), slab_rows, same, spectral, own, pieces, backward, paired)
    met = replica_swap(sent, 1)

    occurs = (offsets[:, None] + jnp.arange(STEPS, dtype=jnp.int32)[None, :]) % blocks
    counts = jnp.sum((occurs[:, :, None] == jnp.arange(blocks, dtype=jnp.int32)).astype(jnp.float32), axis=(0, 1))
    partners = block ^ jnp.stack([met_by[replica], met_by[replica ^ 1]])
    weights = counts[(block - partners) % blocks]
    far = blend(weights, kept, met)
    arrived = replica_swap(far, 2)
    exchanged = blend(weights, kept, met, arrived).reshape(1, cells // replicas)

    others = block ^ jnp.stack(
        [jnp.zeros_like(block), sent_to[replica], sent_to[replica ^ 1], sent_to[(replica ^ 2) // 2 * 2]]
    )
    factors = counts[(others[None, :] - partners[:, None]) % blocks].reshape(-1) / float(NG**3)
    places = jnp.concatenate([others, jnp.stack([(1 - high) * slab_rows, high * slab_rows, low])])
    rows_of = gram(places.astype(jnp.int32), factors, kept, met, own, *pieces, *nears, *evens, *odds)
    rows_of = rows_of + replica_swap(rows_of, 1)
    rows_of = rows_of + replica_swap(rows_of, 2)
    return exchanged, rows_of[:1, :blocks]


def local(orbitals, offsets):
    blocks, replicas = lax.axis_size("blk"), lax.axis_size("rep")
    table = cas_table(NG)
    forward = table.reshape(NG, NG // 2, 2).transpose(0, 2, 1).reshape(NG, NG)
    paired = jnp.kron(jnp.eye(2, dtype=jnp.float32), table)
    tables = screened_kernel(NG), forward, forward.T, paired
    if blocks == replicas == len(MET):
        return folded(orbitals, offsets, tables)
    return stepped(orbitals, offsets, tables)


def solution(mesh):
    placed = (P(("groups", "blk"), None), P("groups"))
    return jax.shard_map(
        local,
        mesh=mesh,
        in_specs=placed,
        out_specs=(P(("groups", "blk"), "rep"), P(("groups", "blk"), None)),
        check_vma=False,
    )
```

```python
import functools

import jax
import jax.numpy as jnp
from jax import lax
from jax.experimental import pallas as pl
from jax.experimental.pallas import tpu as pltpu
from jax.sharding import PartitionSpec as P


NG = 64
STEPS = 3
LANES = 128
HALF = LANES // 2
PITCH = NG + 1
MET = (3, 1, 2, 0)
SENT = (3, 1, 2, 1)
SAME, LOW, HIGH, FAR_SENT, NEAR_SENT, FAR_KEPT, NEAR_KEPT, OWN, OTHERS = 0, 1, 2, 3, 4, 5, 6, 7, 9
screen_scale = 0.05


def passed_along(block, axis, distance):
    devices = range(lax.axis_size(axis))
    route = [((i - distance) % len(devices), i) for i in devices]
    return lax.ppermute(block, axis, route)


def cas_table(grid_points):
    grid_index = jnp.arange(grid_points, dtype=jnp.int32)
    product = grid_index[:, None] * grid_index[None, :] % grid_points
    phase_angle = 2.0 * jnp.pi / grid_points * product.astype(jnp.float32)
    return jnp.cos(phase_angle) + jnp.sin(phase_angle)


def screened_kernel(grid_points):
    def squares(index):
        folded = jnp.where(index <= grid_points // 2, index, index - grid_points).astype(jnp.float32)
        return folded * folded

    shape = (grid_points * grid_points // 2, 2 * grid_points)
    row = lax.broadcasted_iota(jnp.int32, shape, 0)
    lane = lax.broadcasted_iota(jnp.int32, shape, 1)
    k_squared = (
        squares(row % grid_points)
        + squares(2 * (row // grid_points) + lane // grid_points)
        + squares(lane % grid_points)
    )
    safe_square = jnp.maximum(k_squared, 1.0)
    screened = (
        4.0
        * jnp.pi
        / (screen_scale * safe_square)
        * (1.0 - jnp.exp(-screen_scale * safe_square / (4.0 * jnp.pi)))
    )
    return jnp.where(k_squared > 0.5, screened, jnp.ones_like(screened))


def high_low(value):
    high = value.astype(jnp.bfloat16)
    return high, (value - high.astype(jnp.float32)).astype(jnp.bfloat16)


def dot(a, b):
    return lax.dot_general(a, b, (((1,), (0,)), ((), ())), preferred_element_type=jnp.float32)


def swapped(first, second, low_half):
    return (
        jnp.where(low_half, first, pltpu.roll(second, HALF, 1)),
        jnp.where(low_half, pltpu.roll(first, HALF, 1), second),
    )


def left_weights(table):
    high, low = high_low(table)
    return jnp.concatenate([high, high, low], axis=1)


def lane_weights(table):
    high, low = high_low(table)
    return jnp.concatenate(
        [jnp.concatenate([high, low], axis=1), jnp.concatenate([high, jnp.zeros_like(low)], axis=1)],
        axis=0,
    )


def from_left(weights, value):
    high, low = high_low(value)
    return dot(weights, jnp.concatenate([high, low, high], axis=0))


def along_lanes(value, weights):
    high, low = high_low(value)
    both = dot(jnp.concatenate([high, low], axis=1), weights)
    return both[:, :LANES] + both[:, LANES:]


def low_mask(rows):
    return lax.broadcasted_iota(jnp.int32, (rows, LANES), 1) < HALF


def kernel_call(body, shape, spaces, flops, cells, **more):
    memory = {"s": pltpu.SMEM, "v": pltpu.VMEM}
    return pl.pallas_call(
        body,
        out_shape=jax.ShapeDtypeStruct(shape, jnp.float32),
        in_specs=[pl.BlockSpec(memory_space=memory[space]) for space in spaces],
        out_specs=pl.BlockSpec(memory_space=pltpu.VMEM),
        compiler_params=pltpu.CompilerParams(vmem_limit_bytes=24 << 20),
        cost_estimate=pl.CostEstimate(flops=flops, bytes_accessed=4 * cells, transcendentals=0),
        **more,
    )


def planes_body(places, factors, own, visiting, forward, paired, out, *, first_row):
    plane = NG // 2
    mask = low_mask(plane)
    w_forward = left_weights(forward[...])
    w_lanes = lane_weights(paired[...])
    alone = places[SAME] == 1

    def planes(step, _):
        at = pl.multiple_of(step * (4 * plane), 4 * plane)
        mine = own[pl.ds(first_row + at, 4 * plane), :]
        density = mine * jnp.where(alone, mine, visiting[pl.ds(at, 4 * plane), :])
        along_z = along_lanes(density, w_lanes)
        blocks = []
        for half in range(2):
            base = half * 2 * plane
            even, odd = swapped(along_z[base : base + plane], along_z[base + plane : base + 2 * plane], mask)
            blocks.append(jnp.concatenate([even, odd], axis=0))
        along_y = from_left(w_forward, jnp.concatenate(blocks, axis=1))
        out[pl.ds(step * (2 * PITCH), NG), :] = along_y[:, :LANES]
        out[pl.ds(step * (2 * PITCH) + PITCH, NG), :] = along_y[:, LANES:]
        return 0

    steps = visiting.shape[0] // (4 * plane)
    lax.fori_loop(0, steps, planes, 0, unroll=steps)


def columns_body(head, kernel, forward, backward, tail, out):
    plane = NG // 2
    pairs = NG // 4
    mask = low_mask(plane)
    w_forward = left_weights(forward[...])
    w_backward = left_weights(backward[...])

    def columns(step, _):
        blocks = []
        for part in range(2):
            row = 4 * step + 2 * part
            first, second = (
                jnp.concatenate([half[pl.ds(row + odd, pairs, stride=PITCH), :] for half in (head, tail)], axis=0)
                for odd in range(2)
            )
            blocks.append(jnp.concatenate(swapped(first, second, mask), axis=0))
        along_x = from_left(w_forward, jnp.concatenate(blocks, axis=1))
        at = pl.multiple_of(step * (2 * NG), 2 * NG)
        weight = jnp.concatenate([kernel[pl.ds(at, NG), :], kernel[pl.ds(at + NG, NG), :]], axis=1)
        returned = from_left(w_backward, along_x * weight)
        for part in range(2):
            block = returned[:, part * LANES : (part + 1) * LANES]
            row = 4 * step + 2 * part
            for odd, value in enumerate(swapped(block[:plane], block[plane:], mask)):
                out[pl.ds(row + odd, plane, stride=PITCH), :] = value
        return 0

    lax.fori_loop(0, NG // 4, columns, 0, unroll=NG // 4)


def last_body(places, factors, head, own, visiting, kernel, forward, backward, paired, out, tail, *, first_row):
    planes_body(places, factors, own, visiting, forward, paired, tail, first_row=first_row)
    columns_body(head, kernel, forward, backward, tail, out)


def first_planes(places, factors, own, visiting, forward, paired):
    rows = visiting.shape[0]
    return kernel_call(
        functools.partial(planes_body, first_row=0),
        (rows // NG * PITCH, LANES),
        "ssvvvv",
        rows * LANES * NG * 4,
        3 * rows * LANES,
    )(places, factors, own, visiting, forward, paired)


def spectrum(places, factors, head, own, visiting, kernel, forward, backward, paired):
    rows = visiting.shape[0]
    return kernel_call(
        functools.partial(last_body, first_row=rows),
        (2 * rows // NG * PITCH, LANES),
        "ssvvvvvvv",
        rows * LANES * NG * 20,
        12 * rows * LANES,
        scratch_shapes=[pltpu.VMEM((rows // NG * PITCH, LANES), jnp.float32)],
    )(places, factors, head, own, visiting, kernel, forward, backward, paired)


def term_body(places, spectral, own, even, odd, backward, paired, out, *, which):
    plane = NG // 2
    mask = low_mask(plane)
    w_backward = left_weights(backward[...])
    w_lanes = lane_weights(paired[...])
    slab_rows = out.shape[0]
    start = places[which] * slab_rows
    half_rows = even.shape[0]
    alone = places[SAME] == 1
    later = start >= half_rows
    inside = start % half_rows

    def planes(step, _):
        at = step * (4 * plane)
        row = (start // NG + 2 * step) * PITCH
        pair = jnp.concatenate([spectral[pl.ds(row, NG), :], spectral[pl.ds(row + PITCH, NG), :]], axis=1)
        along_y = from_left(w_backward, pair)
        blocks = []
        for half in range(2):
            block = along_y[:, half * LANES : (half + 1) * LANES]
            blocks.extend(swapped(block[:plane], block[plane:], mask))
        potential = along_lanes(jnp.concatenate(blocks, axis=0), w_lanes)
        near = pl.multiple_of(inside + at, 4 * plane)
        visiting = jnp.where(later, odd[pl.ds(near, 4 * plane), :], even[pl.ds(near, 4 * plane), :])
        partner = jnp.where(alone, own[pl.ds(pl.multiple_of(start + at, 4 * plane), 4 * plane), :], visiting)
        out[pl.ds(pl.multiple_of(at, 4 * plane), 4 * plane), :] = potential * (partner * (1.0 / NG**3))
        return 0

    steps = slab_rows // (4 * plane)
    lax.fori_loop(0, steps, planes, 0, unroll=steps)


def term(which, slab_rows, places, spectral, own, pieces, backward, paired):
    cells = slab_rows * LANES
    return kernel_call(
        functools.partial(term_body, which=which), (slab_rows, LANES), "svvvvvv", cells * NG * 12, 4 * cells
    )(places, spectral, own, *pieces, backward, paired)


def blend_body(factors, kept, met, *refs):
    *more, out = refs
    value = factors[0] * kept[...] + factors[1] * met[...]
    out[...] = value + more[0][...] if more else value


def blend(factors, kept, met, *more):
    cells = kept.size
    return kernel_call(blend_body, kept.shape, "svv" + "v" * len(more), 4 * cells, 4 * cells)(factors, kept, met, *more)


def pick_body(places, mine, near, out):
    out[...] = jnp.where(places[LOW] == 0, mine[...], near[...])


def blocks_call(body, places, arrays, indices, shape, block, flops, scalars=()):
    def spec(index):
        return pl.BlockSpec(block, lambda i, held: (held[int(index)] if isinstance(index, str) else index, 0))

    return pl.pallas_call(
        body,
        out_shape=jax.ShapeDtypeStruct(shape, jnp.float32),
        grid_spec=pltpu.PrefetchScalarGridSpec(
            num_scalar_prefetch=1,
            grid=(1,),
            in_specs=[pl.BlockSpec(memory_space=pltpu.SMEM) for _ in scalars] + [spec(index) for index in indices],
            out_specs=pl.BlockSpec(shape, lambda i, held: (0, 0)),
        ),
        compiler_params=pltpu.CompilerParams(vmem_limit_bytes=24 << 20),
        cost_estimate=pl.CostEstimate(
            flops=flops, bytes_accessed=4 * block[0] * block[1] * len(arrays), transcendentals=0
        ),
    )(places, *scalars, *arrays)


def pick(places, mine, near):
    rows = mine.shape[0] // 2
    return blocks_call(
        pick_body, places, (mine, near), (str(LOW), str(LOW)), (rows, LANES), (rows, LANES), rows * LANES
    )


def gram_body(places, factors, *refs):
    *stores, out = refs
    far, near, sides = stores[0:2], stores[2:4], (stores[4:8], stores[8:12])
    rows = far[0].shape[0]
    chunk = 64

    def folded_rows(value):
        return jnp.sum(value.reshape(chunk // 8, 8, LANES), axis=0)

    totals = (jnp.zeros((8, LANES), jnp.float32),) * 8
    for side in range(2):
        is_near = places[HIGH] == side

        def step(index, totals, side=side, is_near=is_near):
            at = pl.ds(pl.multiple_of(index * chunk, chunk), chunk)
            terms = [jnp.where(is_near, near[t][at, :], far[t][at, :]) for t in range(2)]
            orbitals = [store[at, :] for store in sides[side]]
            return tuple(
                totals[4 * t + o] + folded_rows(terms[t] * orbitals[o]) for t in range(2) for o in range(4)
            )

        totals = lax.fori_loop(0, rows // chunk, step, totals, unroll=2)
    lane = lax.broadcasted_iota(jnp.int32, (8, LANES), 1)
    result = jnp.zeros((8, LANES), jnp.float32)
    for o in range(4):
        value = jnp.sum(factors[2 + o] * totals[o] + factors[6 + o] * totals[4 + o], axis=(0, 1), keepdims=True)
        result = jnp.where(lane == places[OTHERS + o], value, result)
    out[...] = result


def gram(places, factors, far, near, own, pieces, nears, moved):
    rows = far[0].shape[0]
    arrays = list(far) + list(near)
    indices = [0] * 4
    for side in range(2):
        arrays += [own, pieces[side], nears[side], moved[side]]
        indices += [str(OWN + side), str(LOW), str(LOW), 0]
    return blocks_call(gram_body, places, arrays, indices, (8, LANES), (rows, LANES), 32 * rows * LANES, (factors,))


def position_block(orbital_block, amount):
    bit_count = (lax.axis_size("blk") - 1).bit_length()
    for bit_level in range(bit_count):
        moved_block = passed_along(orbital_block, "blk", 1 << bit_level)
        orbital_block = jnp.where(amount // (1 << bit_level) % 2 == 1, moved_block, orbital_block)
    return orbital_block


def stepped(orbitals, offsets, tables):
    blocks, replicas = lax.axis_size("blk"), lax.axis_size("rep")
    replica = lax.axis_index("rep")
    cells = orbitals.shape[1]
    rows = cells // LANES
    kernel, forward, backward, paired = tables
    first = position_block(orbitals, (offsets[replica] + STEPS // 2) % blocks)
    visits = [first]
    for distance in range(1, STEPS // 2 + 1):
        visits.append(passed_along(first, "blk", -distance))
        visits.append(passed_along(first, "blk", distance))
    own = orbitals.reshape(rows, LANES)
    slab_rows = rows // replicas
    places = jnp.zeros((OTHERS,), jnp.int32)
    factors = jnp.zeros((2,), jnp.float32)
    whole = jnp.zeros((rows, LANES), jnp.float32)
    for visit in visits:
        visit = visit.reshape(rows, LANES)
        pieces = visit[: rows // 2], visit[rows // 2 :]
        head = first_planes(places, factors, own, pieces[0], forward, paired)
        spectral = spectrum(places, factors, head, own, pieces[1], kernel, forward, backward, paired)
        slabs = [
            term(FAR_SENT, slab_rows, places.at[FAR_SENT].set(r), spectral, own, pieces, backward, paired)
            for r in range(replicas)
        ]
        whole = whole + jnp.concatenate(slabs, axis=0)
    exchanged = lax.psum_scatter(whole.reshape(1, cells), "rep", scatter_dimension=1, tiled=True)
    quarter = lax.dynamic_slice_in_dim(orbitals, replica * (cells // replicas), cells // replicas, 1)
    slab_orbitals = lax.all_to_all(quarter, "blk", split_axis=1, concat_axis=0, tiled=True)
    slab_exchanged = lax.all_to_all(exchanged, "blk", split_axis=1, concat_axis=0, tiled=True)
    partial_value = lax.dot_general(
        slab_orbitals, slab_exchanged, (((1,), (1,)), ((), ())), precision=lax.Precision.HIGHEST
    ) / float(NG**3)
    gram_rows = lax.psum_scatter(partial_value, "blk", scatter_dimension=0, tiled=True)
    return exchanged, lax.psum(gram_rows, "rep")


def folded(orbitals, offsets, tables):
    blocks, replicas = lax.axis_size("blk"), lax.axis_size("rep")
    block, replica = lax.axis_index("blk"), lax.axis_index("rep")
    low, high = replica % 2, replica // 2
    cells = orbitals.shape[1]
    rows = cells // LANES
    slab_rows = rows // replicas
    kernel, forward, backward, paired = tables
    own = orbitals.reshape(rows, LANES)
    met_by = jnp.asarray(MET, jnp.int32)
    sent_to = jnp.asarray(SENT, jnp.int32)

    partners = block ^ jnp.stack([met_by[replica], met_by[replica ^ 1]])
    others = block ^ jnp.stack(
        [jnp.zeros_like(block), sent_to[replica], sent_to[replica ^ 1], sent_to[(replica ^ 2) // 2 * 2]]
    )
    far_side, near_side = 2 * (1 - high), 2 * high
    sides = [far_side + 1 - low, near_side + 1 - low, far_side + low, near_side + low, low, 2 + low]
    same = (met_by[replica] == 0).astype(jnp.int32)
    places = jnp.concatenate([jnp.stack([same, low, high] + sides), others]).astype(jnp.int32)
    apart = jnp.concatenate([block - partners, (others[None, :] - partners[:, None]).reshape(-1)])
    occurs = offsets[:, None] + jnp.arange(STEPS, dtype=jnp.int32)[None, :]
    hits = (occurs[None] - apart[:, None, None]) % blocks == 0
    factors = jnp.sum(hits.astype(jnp.float32), axis=(1, 2))
    factors = factors * jnp.where(jnp.arange(apart.shape[0]) < 2, 1.0, 1.0 / NG**3)

    def along_blocks(value):
        route = [((b ^ SENT[r]) * replicas + r, b * replicas + r) for b in range(blocks) for r in range(replicas)]
        return lax.ppermute(value, ("blk", "rep"), route)

    def replica_swap(value, bit):
        return lax.ppermute(value, "rep", [(r, r ^ bit) for r in range(replicas)])

    piece_a = along_blocks(own[: rows // 2])
    piece_b = along_blocks(own[rows // 2 :])
    near_a = replica_swap(piece_a, 1)
    moved_a = replica_swap(pick(places, piece_a, near_a), 2)
    head = first_planes(places, factors, own, piece_a, forward, paired)
    near_b = replica_swap(piece_b, 1)
    spectral = spectrum(places, factors, head, own, piece_b, kernel, forward, backward, paired)
    picked_b = pick(places, piece_b, near_b)
    moved_b = replica_swap(picked_b, 2)

    pieces = piece_a, piece_b
    terms = {}
    for which in (FAR_SENT, FAR_KEPT, NEAR_SENT, NEAR_KEPT):
        terms[which] = term(which, slab_rows, places, spectral, own, pieces, backward, paired)
    met_far = replica_swap(terms[FAR_SENT], 1)
    met_near = replica_swap(terms[NEAR_SENT], 1)
    arrived = replica_swap(blend(factors, terms[FAR_KEPT], met_far), 2)
    near_sum = blend(factors, terms[NEAR_KEPT], met_near, arrived)
    row = gram(
        places,
        factors,
        (terms[FAR_KEPT], met_far),
        (terms[NEAR_KEPT], met_near),
        own,
        pieces,
        (near_a, near_b),
        (moved_a, moved_b),
    )
    row = row + replica_swap(row, 1)
    row = row + replica_swap(row, 2)
    return near_sum.reshape(1, cells // replicas), row[:1, :blocks]


def local(orbitals, offsets):
    blocks, replicas = lax.axis_size("blk"), lax.axis_size("rep")
    table = cas_table(NG)
    forward = table.reshape(NG, NG // 2, 2).transpose(0, 2, 1).reshape(NG, NG)
    paired = jnp.kron(jnp.eye(2, dtype=jnp.float32), table)
    tables = screened_kernel(NG), forward, forward.T, paired
    if is_folded(blocks, replicas):
        return folded(orbitals, offsets, tables)
    return stepped(orbitals, offsets, tables)


def is_folded(blocks, replicas):
    return blocks == replicas == len(MET)


def solution(mesh):
    placed = (P(("groups", "blk"), None), P("groups"))
    step = jax.shard_map(
        local,
        mesh=mesh,
        in_specs=placed,
        out_specs=(P(("groups", "blk"), "rep"), P(("groups", "blk"), None)),
        check_vma=False,
    )
    if not is_folded(mesh.shape["blk"], mesh.shape["rep"]):
        return step
    return step
```

```python
import functools

import jax
import jax.numpy as jnp
from jax import lax
from jax.experimental import pallas as pl
from jax.experimental.pallas import tpu as pltpu
from jax.sharding import PartitionSpec as P


NG = 64
STEPS = 3
LANES = 128
HALF = LANES // 2
PITCH = NG + 1
GROUP = 256
MET = (3, 1, 2, 0)
SENT = (3, 1, 2, 1)
SENT_A = (3, 3, 2, 2)
SENT_B = (1, 1, 1, 1)
SLABS = len(MET)
SAME, LOW, HIGH, FAR_SENT, NEAR_SENT, FAR_KEPT, NEAR_KEPT, OWN, OTHERS = 0, 1, 2, 3, 4, 5, 6, 7, 9
screen_scale = 0.05


def passed_along(block, axis, distance):
    devices = range(lax.axis_size(axis))
    route = [((i - distance) % len(devices), i) for i in devices]
    return lax.ppermute(block, axis, route)


def cas_table(grid_points):
    grid_index = jnp.arange(grid_points, dtype=jnp.int32)
    product = grid_index[:, None] * grid_index[None, :] % grid_points
    phase_angle = 2.0 * jnp.pi / grid_points * product.astype(jnp.float32)
    return jnp.cos(phase_angle) + jnp.sin(phase_angle)


def screened_kernel(grid_points):
    def squares(index):
        folded = jnp.where(index <= grid_points // 2, index, index - grid_points).astype(jnp.float32)
        return folded * folded

    shape = (grid_points * grid_points // 2, 2 * grid_points)
    row = lax.broadcasted_iota(jnp.int32, shape, 0)
    lane = lax.broadcasted_iota(jnp.int32, shape, 1)
    k_squared = (
        squares(row % grid_points)
        + squares(2 * (row // grid_points) + lane // grid_points)
        + squares(lane % grid_points)
    )
    safe_square = jnp.maximum(k_squared, 1.0)
    screened = (
        4.0
        * jnp.pi
        / (screen_scale * safe_square)
        * (1.0 - jnp.exp(-screen_scale * safe_square / (4.0 * jnp.pi)))
    )
    return jnp.where(k_squared > 0.5, screened, jnp.ones_like(screened))


def high_low(value):
    high = value.astype(jnp.bfloat16)
    return high, (value - high.astype(jnp.float32)).astype(jnp.bfloat16)


def dot(a, b):
    return lax.dot_general(a, b, (((1,), (0,)), ((), ())), preferred_element_type=jnp.float32)


def swapped(first, second, low_half):
    return (
        jnp.where(low_half, first, pltpu.roll(second, HALF, 1)),
        jnp.where(low_half, pltpu.roll(first, HALF, 1), second),
    )


def left_weights(table):
    high, low = high_low(table)
    return jnp.concatenate([high, high, low], axis=1)


def lane_weights(table):
    high, low = high_low(table)
    return jnp.concatenate(
        [jnp.concatenate([high, low], axis=1), jnp.concatenate([high, jnp.zeros_like(low)], axis=1)],
        axis=0,
    )


def from_left(weights, value):
    high, low = high_low(value)
    return dot(weights, jnp.concatenate([high, low, high], axis=0))


def along_lanes(value, weights):
    high, low = high_low(value)
    both = dot(jnp.concatenate([high, low], axis=1), weights)
    return both[:, :LANES] + both[:, LANES:]


def low_mask(rows):
    return lax.broadcasted_iota(jnp.int32, (rows, LANES), 1) < HALF


def kernel_call(body, shape, spaces, flops, cells, **more):
    memory = {"s": pltpu.SMEM, "v": pltpu.VMEM}
    return pl.pallas_call(
        body,
        out_shape=jax.ShapeDtypeStruct(shape, jnp.float32),
        in_specs=[pl.BlockSpec(memory_space=memory[space]) for space in spaces],
        out_specs=pl.BlockSpec(memory_space=pltpu.VMEM),
        compiler_params=pltpu.CompilerParams(vmem_limit_bytes=24 << 20),
        cost_estimate=pl.CostEstimate(flops=flops, bytes_accessed=4 * cells, transcendentals=0),
        **more,
    )


def weights_body(forward, backward, paired, left_y, left_back, lanes):
    left_y[...] = left_weights(forward[...])
    left_back[...] = left_weights(backward[...])
    lanes[...] = lane_weights(paired[...])


def prepared_weights(forward, backward, paired):
    vmem = pl.BlockSpec(memory_space=pltpu.VMEM)
    shapes = (NG, 3 * NG), (NG, 3 * NG), (2 * LANES, 2 * LANES)
    return pl.pallas_call(
        weights_body,
        out_shape=[jax.ShapeDtypeStruct(shape, jnp.bfloat16) for shape in shapes],
        in_specs=[vmem] * 3,
        out_specs=[vmem] * 3,
        name="weights",
    )(forward, backward, paired)


def planes_body(own, visit_at, alone, left_y, lanes, along_z, out, *, first_row):
    plane = NG // 2
    mask = low_mask(plane)
    w_forward = left_y[...]
    w_lanes = lanes[...]
    rows = along_z.shape[0]
    for at in range(0, rows, GROUP):
        mine = own[first_row + at : first_row + at + GROUP, :]
        density = mine * jnp.where(alone, mine, visit_at(at))
        along_z[at : at + GROUP, :] = along_lanes(density, w_lanes)

    def step_planes(step, _):
        at = step * (4 * plane)
        blocks = []
        for half in range(2):
            base = at + half * 2 * plane
            lines = [along_z[pl.ds(pl.multiple_of(base + odd * plane, plane), plane), :] for odd in range(2)]
            blocks.append(jnp.concatenate(swapped(*lines, mask), axis=0))
        along_y = from_left(w_forward, jnp.concatenate(blocks, axis=1))
        out[pl.ds(step * (2 * PITCH), NG), :] = along_y[:, :LANES]
        out[pl.ds(step * (2 * PITCH) + PITCH, NG), :] = along_y[:, LANES:]
        return 0

    steps = rows // (4 * plane)
    lax.fori_loop(0, steps, step_planes, 0, unroll=steps)


def first_body(places, factors, own, visiting, left_y, lanes, out, along_z):
    def visit_at(at):
        return visiting[at : at + GROUP, :]

    planes_body(own, visit_at, places[SAME] == 1, left_y, lanes, along_z, out, first_row=0)


def spectrum_body(
    places, factors, own, head, low_even, low_odd, high_even, high_odd, kernel, left_y, left_back, lanes, out, late,
    tail, along_z,
):
    plane = NG // 2
    pairs = NG // 4
    mask = low_mask(plane)
    slab_rows = low_even.shape[0]
    even = places[LOW] == 0

    def visit_at(at):
        inside = slice(at % slab_rows, at % slab_rows + GROUP)
        by_parity = (low_even, low_odd) if at < slab_rows else (high_even, high_odd)
        value = jnp.where(even, by_parity[0][inside, :], by_parity[1][inside, :])
        late[at : at + GROUP, :] = value
        return value

    planes_body(own, visit_at, places[SAME] == 1, left_y, lanes, along_z, tail, first_row=2 * slab_rows)
    w_forward = left_y[...]
    w_backward = left_back[...]

    def columns(step, _):
        blocks = []
        for part in range(2):
            row = 4 * step + 2 * part
            first, second = (
                jnp.concatenate([half[pl.ds(row + odd, pairs, stride=PITCH), :] for half in (head, tail)], axis=0)
                for odd in range(2)
            )
            blocks.append(jnp.concatenate(swapped(first, second, mask), axis=0))
        along_x = from_left(w_forward, jnp.concatenate(blocks, axis=1))
        at = pl.multiple_of(step * (2 * NG), 2 * NG)
        weight = jnp.concatenate([kernel[pl.ds(at, NG), :], kernel[pl.ds(at + NG, NG), :]], axis=1)
        returned = from_left(w_backward, along_x * weight)
        for part in range(2):
            block = returned[:, part * LANES : (part + 1) * LANES]
            row = 4 * step + 2 * part
            for odd, value in enumerate(swapped(block[:plane], block[plane:], mask)):
                out[pl.ds(row + odd, plane, stride=PITCH), :] = value
        return 0

    lax.fori_loop(0, NG // 4, columns, 0, unroll=NG // 4)


def first_planes(places, factors, own, visiting, weights):
    left_y, _, lanes = weights
    rows = visiting.shape[0]
    return kernel_call(
        first_body,
        (rows // NG * PITCH, LANES),
        "ssvvvv",
        rows * LANES * NG * 4,
        4 * rows * LANES,
        scratch_shapes=[pltpu.VMEM((rows, LANES), jnp.float32)],
    )(places, factors, own, visiting, left_y, lanes)


def spectrum(places, factors, own, head, quarters, kernel, weights):
    rows = own.shape[0]
    smem = pl.BlockSpec(memory_space=pltpu.SMEM)
    vmem = pl.BlockSpec(memory_space=pltpu.VMEM)
    half = rows // 2
    return pl.pallas_call(
        spectrum_body,
        out_shape=[
            jax.ShapeDtypeStruct((rows // NG * PITCH, LANES), jnp.float32),
            jax.ShapeDtypeStruct((half, LANES), jnp.float32),
        ],
        in_specs=[smem] * 2 + [vmem] * 10,
        out_specs=[vmem] * 2,
        scratch_shapes=[
            pltpu.VMEM((half // NG * PITCH, LANES), jnp.float32),
            pltpu.VMEM((half, LANES), jnp.float32),
        ],
        compiler_params=pltpu.CompilerParams(vmem_limit_bytes=24 << 20),
        cost_estimate=pl.CostEstimate(
            flops=rows * LANES * NG * 10, bytes_accessed=24 * rows * LANES, transcendentals=0
        ),
        name="spectrum",
    )(places, factors, own, head, *quarters, kernel, *weights)


def term_body(places, spectral, own, even, odd, left_back, lanes, out, back_y, *, which):
    plane = NG // 2
    mask = low_mask(plane)
    w_backward = left_back[...]
    w_lanes = lanes[...]
    slab_rows = out.shape[0]
    start = places[which] * slab_rows
    half_rows = even.shape[0]
    alone = places[SAME] == 1
    later = start >= half_rows
    inside = start % half_rows

    def step_planes(step, _):
        at = step * (4 * plane)
        row = (start // NG + 2 * step) * PITCH
        pair = jnp.concatenate([spectral[pl.ds(row, NG), :], spectral[pl.ds(row + PITCH, NG), :]], axis=1)
        along_y = from_left(w_backward, pair)
        for half in range(2):
            block = along_y[:, half * LANES : (half + 1) * LANES]
            for second, value in enumerate(swapped(block[:plane], block[plane:], mask)):
                line = pl.multiple_of(at + (2 * half + second) * plane, plane)
                back_y[pl.ds(line, plane), :] = value
        return 0

    steps = slab_rows // (4 * plane)
    lax.fori_loop(0, steps, step_planes, 0, unroll=steps)
    for at in range(0, slab_rows, GROUP):
        potential = along_lanes(back_y[at : at + GROUP, :], w_lanes)
        near = pl.ds(pl.multiple_of(inside + at, 8), GROUP)
        visiting = jnp.where(later, odd[near, :], even[near, :])
        partner = jnp.where(alone, own[pl.ds(pl.multiple_of(start + at, 8), GROUP), :], visiting)
        out[at : at + GROUP, :] = potential * (partner * (1.0 / NG**3))


def term(which, slab_rows, places, spectral, own, pieces, weights):
    cells = slab_rows * LANES
    return kernel_call(
        functools.partial(term_body, which=which),
        (slab_rows, LANES),
        "svvvvvv",
        cells * NG * 12,
        4 * cells,
        scratch_shapes=[pltpu.VMEM((slab_rows, LANES), jnp.float32)],
    )(places, spectral, own, *pieces, weights[1], weights[2])


def blend_body(factors, kept, met, out):
    out[...] = factors[0] * kept[...] + factors[1] * met[...]


def blend(factors, kept, met):
    return kernel_call(blend_body, kept.shape, "svv", 3 * kept.size, 3 * kept.size)(factors, kept, met)


def join_body(first, second, out):
    out[...] = first[...] + second[...]


def join(first, second):
    return kernel_call(join_body, first.shape, "vv", first.size, 3 * first.size)(first, second)


def pick_body(places, mine, near, out):
    rows = out.shape[0]
    out[...] = jnp.where(places[LOW] == 0, mine[:rows, :], near[rows:, :])


def pick(places, mine, near):
    rows = mine.shape[0] // 2
    return kernel_call(pick_body, (rows, LANES), "svv", rows * LANES, 3 * rows * LANES)(places, mine, near)


def seat_body(offsets, places, factors, *, blocks, replicas):
    block, replica = lax.axis_index("blk"), lax.axis_index("rep")
    low, high = replica % 2, replica // 2

    def listed(numbers, index):
        value = jnp.int32(numbers[0])
        for other in range(1, len(numbers)):
            value = jnp.where(index == other, jnp.int32(numbers[other]), value)
        return value

    partners = [block ^ listed(MET, replica), block ^ listed(MET, replica ^ 1)]
    others = [
        block,
        block ^ listed(SENT, replica),
        block ^ listed(SENT, replica ^ 1),
        block ^ listed(SENT, (replica ^ 2) // 2 * 2),
    ]
    far, near = 2 * (1 - high), 2 * high
    same = (listed(MET, replica) == 0).astype(jnp.int32)
    slabs = [far + 1 - low, near + 1 - low, far + low, near + low, low, 2 + low]
    for index, value in enumerate([same, low, high] + slabs + others):
        places[index] = value.astype(jnp.int32)
    shifts = [(offsets[r] + step) % blocks for r in range(replicas) for step in range(STEPS)]
    apart = [(block - partner, 1.0) for partner in partners]
    apart += [(other - partner, 1.0 / NG**3) for partner in partners for other in others]
    for index, (distance, scale) in enumerate(apart):
        wanted = (distance + blocks) % blocks
        hits = jnp.int32(0)
        for shift in shifts:
            hits += (shift == wanted).astype(jnp.int32)
        factors[index] = hits.astype(jnp.float32) * scale


def seat(offsets, blocks, replicas):
    smem = pl.BlockSpec(memory_space=pltpu.SMEM)
    return pl.pallas_call(
        functools.partial(seat_body, blocks=blocks, replicas=replicas),
        out_shape=[
            jax.ShapeDtypeStruct((OTHERS + 4,), jnp.int32),
            jax.ShapeDtypeStruct((10,), jnp.float32),
        ],
        in_specs=[smem],
        out_specs=[smem] * 2,
        name="seat",
    )(offsets)


def gram_body(places, factors, far, met_far, near, met_near, own, *refs):
    piece_a, near_a, moved_a, late_a, late_b, moved_b, out = refs
    even = places[LOW] == 0
    rows = far.shape[0]
    chunk = 64

    def folded_rows(value):
        return jnp.sum(value.reshape(chunk // 8, 8, LANES), axis=0)

    totals = (jnp.zeros((8, LANES), jnp.float32),) * 8
    for side in range(2):
        is_near = places[HIGH] == side
        parity_row = places[LOW] * rows
        own_row = places[OWN + side] * rows

        def step(index, totals, side=side, is_near=is_near, parity_row=parity_row, own_row=own_row):
            inside = index * chunk
            at = pl.ds(pl.multiple_of(inside, chunk), chunk)
            half = pl.ds(pl.multiple_of(parity_row + inside, chunk), chunk)
            mine = pl.ds(pl.multiple_of(own_row + inside, chunk), chunk)
            terms = (
                jnp.where(is_near, near[at, :], far[at, :]),
                jnp.where(is_near, met_near[at, :], met_far[at, :]),
            )
            if side == 0:
                orbitals = (own[mine, :], piece_a[half, :], near_a[half, :], moved_a[at, :])
            else:
                of_a, of_b = late_a[at, :], late_b[at, :]
                orbitals = (own[mine, :], jnp.where(even, of_a, of_b), jnp.where(even, of_b, of_a), moved_b[at, :])
            return tuple(
                totals[4 * t + o] + folded_rows(terms[t] * orbitals[o]) for t in range(2) for o in range(4)
            )

        totals = lax.fori_loop(0, rows // chunk, step, totals, unroll=4)
    lane = lax.broadcasted_iota(jnp.int32, (8, LANES), 1)
    result = jnp.zeros((8, LANES), jnp.float32)
    for o in range(4):
        value = jnp.sum(factors[2 + o] * totals[o] + factors[6 + o] * totals[4 + o], axis=(0, 1), keepdims=True)
        result = jnp.where(lane == places[OTHERS + o], value, result)
    out[...] = result


def gram(places, factors, far, near, own, *stores):
    cells = far[0].size
    return kernel_call(
        gram_body, (8, LANES), "ssvvvvv" + "v" * len(stores), 32 * cells, 12 * cells
    )(places, factors, *far, *near, own, *stores)


def position_block(orbital_block, amount):
    bit_count = (lax.axis_size("blk") - 1).bit_length()
    for bit_level in range(bit_count):
        moved_block = passed_along(orbital_block, "blk", 1 << bit_level)
        orbital_block = jnp.where(amount // (1 << bit_level) % 2 == 1, moved_block, orbital_block)
    return orbital_block


def stepped(orbitals, offsets, tables):
    blocks, replicas = lax.axis_size("blk"), lax.axis_size("rep")
    replica = lax.axis_index("rep")
    cells = orbitals.shape[1]
    rows = cells // LANES
    weights = prepared_weights(*tables)
    kernel = screened_kernel(NG)
    first = position_block(orbitals, (offsets[replica] + STEPS // 2) % blocks)
    visits = [first]
    for distance in range(1, STEPS // 2 + 1):
        visits.append(passed_along(first, "blk", -distance))
        visits.append(passed_along(first, "blk", distance))
    own = orbitals.reshape(rows, LANES)
    places = jnp.zeros((OTHERS,), jnp.int32)
    factors = jnp.zeros((2,), jnp.float32)
    whole = jnp.zeros((rows, LANES), jnp.float32)
    for visit in visits:
        visit = visit.reshape(rows, LANES)
        pieces = visit[: rows // 2], visit[rows // 2 :]
        head = first_planes(places, factors, own, pieces[0], weights)
        quarters = [pieces[1][at : at + rows // SLABS] for at in (0, 0, rows // SLABS, rows // SLABS)]
        spectral, _ = spectrum(places, factors, own, head, quarters, kernel, weights)
        slabs = [
            term(FAR_SENT, rows // SLABS, places.at[FAR_SENT].set(slab), spectral, own, pieces, weights)
            for slab in range(SLABS)
        ]
        whole = whole + jnp.concatenate(slabs, axis=0)
    exchanged = lax.psum_scatter(whole.reshape(1, cells), "rep", scatter_dimension=1, tiled=True)
    quarter = lax.dynamic_slice_in_dim(orbitals, replica * (cells // replicas), cells // replicas, 1)
    slab_orbitals = lax.all_to_all(quarter, "blk", split_axis=1, concat_axis=0, tiled=True)
    slab_exchanged = lax.all_to_all(exchanged, "blk", split_axis=1, concat_axis=0, tiled=True)
    partial_value = lax.dot_general(
        slab_orbitals, slab_exchanged, (((1,), (1,)), ((), ())), precision=lax.Precision.HIGHEST
    ) / float(NG**3)
    gram_rows = lax.psum_scatter(partial_value, "blk", scatter_dimension=0, tiled=True)
    return exchanged, lax.psum(gram_rows, "rep")


def folded(orbitals, offsets, tables):
    blocks, replicas = lax.axis_size("blk"), lax.axis_size("rep")
    replica = lax.axis_index("rep")
    cells = orbitals.shape[1]
    rows = cells // LANES
    slab_rows = rows // replicas
    weights = prepared_weights(*tables)
    own = orbitals.reshape(rows, LANES)
    low = replica % 2
    places, factors = seat(offsets, blocks, replicas)

    def along_blocks(value, sent):
        route = [((b ^ sent[r]) * replicas + r, b * replicas + r) for b in range(blocks) for r in range(replicas)]
        return lax.ppermute(value, ("blk", "rep"), route)

    def replica_swap(value, bit):
        return lax.ppermute(value, "rep", [(r, r ^ bit) for r in range(replicas)])

    def slab_of(index):
        return lax.dynamic_slice_in_dim(own, index * slab_rows, slab_rows, 0)

    piece_a = along_blocks(own[: 2 * slab_rows], SENT)
    late_b = along_blocks(slab_of(3 - low), SENT_B)
    late_a = along_blocks(slab_of(2 + low), SENT_A)

    near_a = replica_swap(piece_a, 1)

    moved_a = replica_swap(pick(places, piece_a, near_a), 2)
    kernel = screened_kernel(NG)
    head = first_planes(places, factors, own, piece_a, weights)
    near_late_b = replica_swap(late_b, 1)
    near_late_a = replica_swap(late_a, 1)
    moved_b = replica_swap(late_a, 2)
    quarters = late_a, late_b, near_late_a, near_late_b
    spectral, piece_b = spectrum(places, factors, own, head, quarters, kernel, weights)
    pieces = piece_a, piece_b
    terms = {}
    for which in (FAR_SENT, FAR_KEPT, NEAR_SENT, NEAR_KEPT):
        terms[which] = term(which, slab_rows, places, spectral, own, pieces, weights)
    met_far = replica_swap(terms[FAR_SENT], 1)
    met_near = replica_swap(terms[NEAR_SENT], 1)

    arrived = replica_swap(blend(factors, terms[FAR_KEPT], met_far), 2)
    row = gram(
        places,
        factors,
        (terms[FAR_KEPT], met_far),
        (terms[NEAR_KEPT], met_near),
        own,
        piece_a,
        near_a,
        moved_a,
        late_a,
        near_late_b,
        moved_b,
    )
    near_sum = blend(factors, terms[NEAR_KEPT], met_near)
    row = row + replica_swap(row, 1)
    other = replica_swap(row, 2)
    margin = row[:1, :blocks] + other[:1, :blocks]
    exchanged = join(near_sum, arrived)
    return exchanged.reshape(1, cells // replicas), margin


def local(orbitals, offsets):
    blocks, replicas = lax.axis_size("blk"), lax.axis_size("rep")
    table = cas_table(NG)
    forward = table.reshape(NG, NG // 2, 2).transpose(0, 2, 1).reshape(NG, NG)
    paired = jnp.kron(jnp.eye(2, dtype=jnp.float32), table)
    tables = forward, forward.T, paired
    if is_folded(blocks, replicas):
        return folded(orbitals, offsets, tables)
    return stepped(orbitals, offsets, tables)


def is_folded(blocks, replicas):
    return blocks == replicas == len(MET)


def solution(mesh):
    placed = (P(("groups", "blk"), None), P("groups"))
    step = jax.shard_map(
        local,
        mesh=mesh,
        in_specs=placed,
        out_specs=(P(("groups", "blk"), "rep"), P(("groups", "blk"), None)),
        check_vma=False,
    )
    if not is_folded(mesh.shape["blk"], mesh.shape["rep"]):
        return step
    return step
```

```python
import functools

import jax
import jax.numpy as jnp
from jax import lax
from jax.experimental import pallas as pl
from jax.experimental.pallas import tpu as pltpu
from jax.sharding import PartitionSpec as P


NG = 64
STEPS = 3
LANES = 128
HALF = LANES // 2
PITCH = NG + 1
GROUP = 256
MET = (3, 1, 2, 0)
SENT = (3, 1, 2, 1)
SENT_A = (3, 3, 2, 2)
SENT_B = (1, 1, 1, 1)
SLABS = len(MET)
SAME, LOW, HIGH, FAR_SENT, NEAR_SENT, FAR_KEPT, NEAR_KEPT, OWN, OTHERS = 0, 1, 2, 3, 4, 5, 6, 7, 9
screen_scale = 0.05


def passed_along(block, axis, distance):
    devices = range(lax.axis_size(axis))
    route = [((i - distance) % len(devices), i) for i in devices]
    return lax.ppermute(block, axis, route)


def cas_table(grid_points):
    grid_index = jnp.arange(grid_points, dtype=jnp.int32)
    product = grid_index[:, None] * grid_index[None, :] % grid_points
    phase_angle = 2.0 * jnp.pi / grid_points * product.astype(jnp.float32)
    return jnp.cos(phase_angle) + jnp.sin(phase_angle)


def screened_kernel(grid_points):
    def squares(index):
        folded = jnp.where(index <= grid_points // 2, index, index - grid_points).astype(jnp.float32)
        return folded * folded

    shape = (grid_points * grid_points // 2, 2 * grid_points)
    row = lax.broadcasted_iota(jnp.int32, shape, 0)
    lane = lax.broadcasted_iota(jnp.int32, shape, 1)
    k_squared = (
        squares(row % grid_points)
        + squares(2 * (row // grid_points) + lane // grid_points)
        + squares(lane % grid_points)
    )
    safe_square = jnp.maximum(k_squared, 1.0)
    screened = (
        4.0
        * jnp.pi
        / (screen_scale * safe_square)
        * (1.0 - jnp.exp(-screen_scale * safe_square / (4.0 * jnp.pi)))
    )
    return jnp.where(k_squared > 0.5, screened, jnp.ones_like(screened))


def high_low(value):
    high = value.astype(jnp.bfloat16)
    return high, (value - high.astype(jnp.float32)).astype(jnp.bfloat16)


def dot(a, b):
    return lax.dot_general(a, b, (((1,), (0,)), ((), ())), preferred_element_type=jnp.float32)


def swapped(first, second, low_half):
    return (
        jnp.where(low_half, first, pltpu.roll(second, HALF, 1)),
        jnp.where(low_half, pltpu.roll(first, HALF, 1), second),
    )


def left_weights(table):
    high, low = high_low(table)
    return jnp.concatenate([high, high, low], axis=1)


def lane_weights(table):
    high, low = high_low(table)
    return jnp.concatenate(
        [jnp.concatenate([high, low], axis=1), jnp.concatenate([high, jnp.zeros_like(low)], axis=1)],
        axis=0,
    )


def from_left(weights, value):
    high, low = high_low(value)
    return dot(weights, jnp.concatenate([high, low, high], axis=0))


def along_lanes(value, weights):
    high, low = high_low(value)
    both = dot(jnp.concatenate([high, low], axis=1), weights)
    return both[:, :LANES] + both[:, LANES:]


def low_mask(rows):
    return lax.broadcasted_iota(jnp.int32, (rows, LANES), 1) < HALF


def kernel_call(body, shape, spaces, flops, cells, **more):
    memory = {"s": pltpu.SMEM, "v": pltpu.VMEM}
    return pl.pallas_call(
        body,
        out_shape=jax.ShapeDtypeStruct(shape, jnp.float32),
        in_specs=[pl.BlockSpec(memory_space=memory[space]) for space in spaces],
        out_specs=pl.BlockSpec(memory_space=pltpu.VMEM),
        compiler_params=pltpu.CompilerParams(vmem_limit_bytes=24 << 20),
        cost_estimate=pl.CostEstimate(flops=flops, bytes_accessed=4 * cells, transcendentals=0),
        **more,
    )


def weights_body(forward, backward, paired, left_y, left_back, lanes):
    left_y[...] = left_weights(forward[...])
    left_back[...] = left_weights(backward[...])
    lanes[...] = lane_weights(paired[...])


def prepared_weights(forward, backward, paired):
    vmem = pl.BlockSpec(memory_space=pltpu.VMEM)
    shapes = (NG, 3 * NG), (NG, 3 * NG), (2 * LANES, 2 * LANES)
    return pl.pallas_call(
        weights_body,
        out_shape=[jax.ShapeDtypeStruct(shape, jnp.bfloat16) for shape in shapes],
        in_specs=[vmem] * 3,
        out_specs=[vmem] * 3,
        name="weights",
    )(forward, backward, paired)


def planes_body(own, visit_at, alone, left_y, lanes, along_z, out, *, first_row):
    plane = NG // 2
    mask = low_mask(plane)
    w_forward = left_y[...]
    w_lanes = lanes[...]
    rows = along_z.shape[0]
    for at in range(0, rows, GROUP):
        mine = own[first_row + at : first_row + at + GROUP, :]
        density = mine * jnp.where(alone, mine, visit_at(at))
        along_z[at : at + GROUP, :] = along_lanes(density, w_lanes)

    def step_planes(step, _):
        at = step * (4 * plane)
        blocks = []
        for half in range(2):
            base = at + half * 2 * plane
            lines = [along_z[pl.ds(pl.multiple_of(base + odd * plane, plane), plane), :] for odd in range(2)]
            blocks.append(jnp.concatenate(swapped(*lines, mask), axis=0))
        along_y = from_left(w_forward, jnp.concatenate(blocks, axis=1))
        out[pl.ds(step * (2 * PITCH), NG), :] = along_y[:, :LANES]
        out[pl.ds(step * (2 * PITCH) + PITCH, NG), :] = along_y[:, LANES:]
        return 0

    steps = rows // (4 * plane)
    lax.fori_loop(0, steps, step_planes, 0, unroll=steps)


def slabs_body(places, own, choices, left_y, lanes, along_z, out, partner, *, first_slab):
    slab_rows = choices[0].shape[0]
    even = places[LOW] == 0
    alone = places[SAME] == 1
    first_row = first_slab * slab_rows

    def visit_at(at):
        inside = slice(at % slab_rows, at % slab_rows + GROUP)
        index = at // slab_rows * 2
        value = jnp.where(even, choices[index][inside, :], choices[index + 1][inside, :])
        partner[at : at + GROUP, :] = jnp.where(alone, own[first_row + at : first_row + at + GROUP, :], value)
        return value

    planes_body(own, visit_at, alone, left_y, lanes, along_z, out, first_row=first_row)


def first_body(places, factors, own, *refs, first_slab, count):
    choices, (left_y, lanes, out, partner, along_z) = refs[: 2 * count], refs[2 * count :]
    slabs_body(places, own, choices, left_y, lanes, along_z, out, partner, first_slab=first_slab)


def spectrum_body(places, factors, own, *refs, heads, first_slab, count):
    parts, choices, rest = refs[:heads], refs[heads : heads + 2 * count], refs[heads + 2 * count :]
    kernel, left_y, left_back, lanes, out, partner, tail, along_z = rest
    plane = NG // 2
    mask = low_mask(plane)
    slabs_body(places, own, choices, left_y, lanes, along_z, tail, partner, first_slab=first_slab)
    parts = (*parts, tail)
    w_forward = left_y[...]
    w_backward = left_back[...]

    def columns(step, _):
        blocks = []
        for part in range(2):
            row = 4 * step + 2 * part
            first, second = (
                jnp.concatenate(
                    [ref[pl.ds(row + odd, ref.shape[0] // PITCH, stride=PITCH), :] for ref in parts], axis=0
                )
                for odd in range(2)
            )
            blocks.append(jnp.concatenate(swapped(first, second, mask), axis=0))
        along_x = from_left(w_forward, jnp.concatenate(blocks, axis=1))
        at = pl.multiple_of(step * (2 * NG), 2 * NG)
        weight = jnp.concatenate([kernel[pl.ds(at, NG), :], kernel[pl.ds(at + NG, NG), :]], axis=1)
        returned = from_left(w_backward, along_x * weight)
        for part in range(2):
            block = returned[:, part * LANES : (part + 1) * LANES]
            row = 4 * step + 2 * part
            for odd, value in enumerate(swapped(block[:plane], block[plane:], mask)):
                out[pl.ds(row + odd, plane, stride=PITCH), :] = value
        return 0

    lax.fori_loop(0, NG // 4, columns, 0, unroll=NG // 4)


def planes_call(body, spaces, planes_rows, partner_rows, scratch_rows, flops, cells):
    smem = pl.BlockSpec(memory_space=pltpu.SMEM)
    vmem = pl.BlockSpec(memory_space=pltpu.VMEM)
    return pl.pallas_call(
        body,
        out_shape=[jax.ShapeDtypeStruct((rows, LANES), jnp.float32) for rows in (planes_rows, partner_rows)],
        in_specs=[smem] * 2 + [vmem] * spaces,
        out_specs=[vmem] * 2,
        scratch_shapes=[pltpu.VMEM((rows, LANES), jnp.float32) for rows in scratch_rows],
        compiler_params=pltpu.CompilerParams(vmem_limit_bytes=24 << 20),
        cost_estimate=pl.CostEstimate(flops=flops, bytes_accessed=4 * cells, transcendentals=0),
    )


def first_planes(first_slab, places, factors, own, choices, weights):
    left_y, _, lanes = weights
    count = len(choices) // 2
    rows = count * choices[0].shape[0]
    body = functools.partial(first_body, first_slab=first_slab, count=count)
    pitched = rows // NG * PITCH
    return planes_call(
        body, 3 + 2 * count, pitched, rows, (rows,), rows * LANES * NG * 4, 4 * rows * LANES
    )(places, factors, own, *choices, left_y, lanes)


def spectrum(first_slab, places, factors, own, heads, choices, kernel, weights):
    count = len(choices) // 2
    rows, last = own.shape[0], count * choices[0].shape[0]
    body = functools.partial(spectrum_body, heads=len(heads), first_slab=first_slab, count=count)
    pitched = rows // NG * PITCH, last // NG * PITCH
    return planes_call(
        body, 5 + len(heads) + 2 * count, pitched[0], last, (pitched[1], last), rows * LANES * NG * 10, 6 * rows * LANES
    )(places, factors, own, *heads, *choices, kernel, *weights)


def terms_body(places, spectral, *refs, which):
    partners, (left_back, lanes, *outs, back_y) = refs[: -3 - len(which)], refs[-3 - len(which) :]
    plane = NG // 2
    mask = low_mask(plane)
    w_backward = left_back[...]
    w_lanes = lanes[...]
    slab_rows = outs[0].shape[0]
    steps = slab_rows // (4 * plane)

    def partner_at(slab, at):
        value, first_slab = None, 0
        for piece in partners:
            count = piece.shape[0] // slab_rows
            row = jnp.clip(slab - first_slab, 0, count - 1) * slab_rows + at
            here = piece[pl.ds(pl.multiple_of(row, 8), GROUP), :]
            value = here if value is None else jnp.where(slab >= first_slab, here, value)
            first_slab += count
        return value

    for index, entry in enumerate(which):
        start = places[entry] * slab_rows
        for step in range(steps):
            row = (start // NG + 2 * step) * PITCH
            pair = jnp.concatenate([spectral[pl.ds(row, NG), :], spectral[pl.ds(row + PITCH, NG), :]], axis=1)
            along_y = from_left(w_backward, pair)
            for half in range(2):
                block = along_y[:, half * LANES : (half + 1) * LANES]
                for second, value in enumerate(swapped(block[:plane], block[plane:], mask)):
                    line = index * slab_rows + (4 * step + 2 * half + second) * plane
                    back_y[line : line + plane, :] = value
    for index, entry in enumerate(which):
        for at in range(0, slab_rows, GROUP):
            line = index * slab_rows + at
            potential = along_lanes(back_y[line : line + GROUP, :], w_lanes)
            outs[index][at : at + GROUP, :] = potential * (partner_at(places[entry], at) * (1.0 / NG**3))


def exchange_terms(which, slab_rows, places, spectral, partners, weights):
    cells = len(which) * slab_rows * LANES
    vmem = pl.BlockSpec(memory_space=pltpu.VMEM)
    return pl.pallas_call(
        functools.partial(terms_body, which=which),
        out_shape=[jax.ShapeDtypeStruct((slab_rows, LANES), jnp.float32) for _ in which],
        in_specs=[pl.BlockSpec(memory_space=pltpu.SMEM)] + [vmem] * (3 + len(partners)),
        out_specs=[vmem] * len(which),
        scratch_shapes=[pltpu.VMEM((len(which) * slab_rows, LANES), jnp.float32)],
        compiler_params=pltpu.CompilerParams(vmem_limit_bytes=24 << 20),
        cost_estimate=pl.CostEstimate(flops=cells * NG * 12, bytes_accessed=16 * cells, transcendentals=0),
        name="terms",
    )(places, spectral, *partners, weights[1], weights[2])


def blend_body(factors, kept, met, out):
    out[...] = factors[0] * kept[...] + factors[1] * met[...]


def blend(factors, kept, met):
    return kernel_call(blend_body, kept.shape, "svv", 3 * kept.size, 3 * kept.size)(factors, kept, met)


def finish_body(near_sum, arrived, row, other, exchanged, margin):
    exchanged[...] = near_sum[...] + arrived[...]
    margin[...] = (row[...] + other[...])[:1, : margin.shape[1]]


def finish(near_sum, arrived, row, other, columns):
    vmem = pl.BlockSpec(memory_space=pltpu.VMEM)
    return pl.pallas_call(
        finish_body,
        out_shape=[
            jax.ShapeDtypeStruct(near_sum.shape, jnp.float32),
            jax.ShapeDtypeStruct((1, columns), jnp.float32),
        ],
        in_specs=[vmem] * 4,
        out_specs=[vmem] * 2,
        compiler_params=pltpu.CompilerParams(vmem_limit_bytes=24 << 20),
        cost_estimate=pl.CostEstimate(
            flops=near_sum.size, bytes_accessed=12 * near_sum.size, transcendentals=0
        ),
        name="finish",
    )(near_sum, arrived, row, other)


def seat_body(offsets, places, factors, *, blocks, replicas):
    block, replica = lax.axis_index("blk"), lax.axis_index("rep")
    low, high = replica % 2, replica // 2

    def listed(numbers, index):
        value = jnp.int32(numbers[0])
        for other in range(1, len(numbers)):
            value = jnp.where(index == other, jnp.int32(numbers[other]), value)
        return value

    partners = [block ^ listed(MET, replica), block ^ listed(MET, replica ^ 1)]
    others = [
        block,
        block ^ listed(SENT, replica),
        block ^ listed(SENT, replica ^ 1),
        block ^ listed(SENT, (replica ^ 2) // 2 * 2),
    ]
    far, near = 2 * (1 - high), 2 * high
    same = (listed(MET, replica) == 0).astype(jnp.int32)
    slabs = [far + 1 - low, near + 1 - low, far + low, near + low, low, 2 + low]
    for index, value in enumerate([same, low, high] + slabs + others):
        places[index] = value.astype(jnp.int32)
    shifts = [(offsets[r] + step) % blocks for r in range(replicas) for step in range(STEPS)]
    apart = [(block - partner, 1.0) for partner in partners]
    apart += [(other - partner, 1.0 / NG**3) for partner in partners for other in others]
    for index, (distance, scale) in enumerate(apart):
        wanted = (distance + blocks) % blocks
        hits = jnp.int32(0)
        for shift in shifts:
            hits += (shift == wanted).astype(jnp.int32)
        factors[index] = hits.astype(jnp.float32) * scale


def seat(offsets, blocks, replicas):
    smem = pl.BlockSpec(memory_space=pltpu.SMEM)
    return pl.pallas_call(
        functools.partial(seat_body, blocks=blocks, replicas=replicas),
        out_shape=[
            jax.ShapeDtypeStruct((OTHERS + 4,), jnp.int32),
            jax.ShapeDtypeStruct((10,), jnp.float32),
        ],
        in_specs=[smem],
        out_specs=[smem] * 2,
        name="seat",
    )(offsets)


def gram_body(places, factors, far, met_far, near, met_near, own, *refs):
    *stores, out = refs
    even = places[LOW] == 0
    rows = far.shape[0]
    chunk = 64

    def folded_rows(value):
        return jnp.sum(value.reshape(chunk // 8, 8, LANES), axis=0)

    totals = (jnp.zeros((8, LANES), jnp.float32),) * 8
    for side in range(2):
        is_near = places[HIGH] == side
        piece_a, near_b, moved_a = stores[3 * side : 3 * side + 3]
        own_row = places[OWN + side] * rows

        def step(index, totals, is_near=is_near, piece_a=piece_a, near_b=near_b, moved_a=moved_a, own_row=own_row):
            inside = index * chunk
            at = pl.ds(pl.multiple_of(inside, chunk), chunk)
            mine = pl.ds(pl.multiple_of(own_row + inside, chunk), chunk)
            terms = (
                jnp.where(is_near, near[at, :], far[at, :]),
                jnp.where(is_near, met_near[at, :], met_far[at, :]),
            )
            of_a, of_b = piece_a[at, :], near_b[at, :]
            orbitals = (own[mine, :], jnp.where(even, of_a, of_b), jnp.where(even, of_b, of_a), moved_a[at, :])
            return tuple(
                totals[4 * t + o] + folded_rows(terms[t] * orbitals[o]) for t in range(2) for o in range(4)
            )

        totals = lax.fori_loop(0, rows // chunk, step, totals, unroll=4)
    lane = lax.broadcasted_iota(jnp.int32, (8, LANES), 1)
    result = jnp.zeros((8, LANES), jnp.float32)
    for o in range(4):
        value = jnp.sum(factors[2 + o] * totals[o] + factors[6 + o] * totals[4 + o], axis=(0, 1), keepdims=True)
        result = jnp.where(lane == places[OTHERS + o], value, result)
    out[...] = result


def gram(places, factors, far, near, own, *stores):
    cells = far[0].size
    return kernel_call(
        gram_body, (8, LANES), "ssvvvvv" + "v" * len(stores), 32 * cells, 12 * cells
    )(places, factors, *far, *near, own, *stores)


def position_block(orbital_block, amount):
    bit_count = (lax.axis_size("blk") - 1).bit_length()
    for bit_level in range(bit_count):
        moved_block = passed_along(orbital_block, "blk", 1 << bit_level)
        orbital_block = jnp.where(amount // (1 << bit_level) % 2 == 1, moved_block, orbital_block)
    return orbital_block


def stepped(orbitals, offsets, tables):
    blocks, replicas = lax.axis_size("blk"), lax.axis_size("rep")
    replica = lax.axis_index("rep")
    cells = orbitals.shape[1]
    rows = cells // LANES
    weights = prepared_weights(*tables)
    kernel = screened_kernel(NG)
    first = position_block(orbitals, (offsets[replica] + STEPS // 2) % blocks)
    visits = [first]
    for distance in range(1, STEPS // 2 + 1):
        visits.append(passed_along(first, "blk", -distance))
        visits.append(passed_along(first, "blk", distance))
    own = orbitals.reshape(rows, LANES)
    places = jnp.zeros((OTHERS,), jnp.int32)
    factors = jnp.zeros((2,), jnp.float32)
    whole = jnp.zeros((rows, LANES), jnp.float32)
    for visit in visits:
        visit = visit.reshape(rows, LANES)
        slab_rows = rows // SLABS
        slabs = [visit[slab * slab_rows : (slab + 1) * slab_rows] for slab in range(SLABS)]
        choices = [slabs[index // 2] for index in range(2 * SLABS)]
        head, partner_a = first_planes(0, places, factors, own, choices[:4], weights)
        spectral, partner_b = spectrum(2, places, factors, own, (head,), choices[4:], kernel, weights)
        numbers = jnp.arange(SLABS, dtype=jnp.int32)
        spots = places.at[FAR_SENT : FAR_SENT + SLABS].set(numbers)
        which = tuple(range(FAR_SENT, FAR_SENT + SLABS))
        terms = exchange_terms(which, slab_rows, spots, spectral, (partner_a, partner_b), weights)
        whole = whole + jnp.concatenate(terms, axis=0)
    exchanged = lax.psum_scatter(whole.reshape(1, cells), "rep", scatter_dimension=1, tiled=True)
    quarter = lax.dynamic_slice_in_dim(orbitals, replica * (cells // replicas), cells // replicas, 1)
    slab_orbitals = lax.all_to_all(quarter, "blk", split_axis=1, concat_axis=0, tiled=True)
    slab_exchanged = lax.all_to_all(exchanged, "blk", split_axis=1, concat_axis=0, tiled=True)
    partial_value = lax.dot_general(
        slab_orbitals, slab_exchanged, (((1,), (1,)), ((), ())), precision=lax.Precision.HIGHEST
    ) / float(NG**3)
    gram_rows = lax.psum_scatter(partial_value, "blk", scatter_dimension=0, tiled=True)
    return exchanged, lax.psum(gram_rows, "rep")


def folded(orbitals, offsets, tables):
    blocks, replicas = lax.axis_size("blk"), lax.axis_size("rep")
    replica = lax.axis_index("rep")
    cells = orbitals.shape[1]
    rows = cells // LANES
    slab_rows = rows // replicas
    weights = prepared_weights(*tables)
    own = orbitals.reshape(rows, LANES)
    low = replica % 2
    places, factors = seat(offsets, blocks, replicas)

    def along_blocks(value, sent):
        route = [((b ^ sent[r]) * replicas + r, b * replicas + r) for b in range(blocks) for r in range(replicas)]
        return lax.ppermute(value, ("blk", "rep"), route)

    def replica_swap(value, bit):
        return lax.ppermute(value, "rep", [(r, r ^ bit) for r in range(replicas)])

    def slab_of(index):
        return lax.dynamic_slice_in_dim(own, index * slab_rows, slab_rows, 0)

    a_first = along_blocks(slab_of(low), SENT_A)
    b_first = along_blocks(slab_of(1 - low), SENT_B)
    b_last = along_blocks(slab_of(3 - low), SENT_B)
    a_last = along_blocks(slab_of(2 + low), SENT_A)
    kernel = screened_kernel(NG)

    near_a_first = replica_swap(a_first, 1)
    near_b_first = replica_swap(b_first, 1)
    moved_first = replica_swap(a_first, 2)
    head, partner = first_planes(
        0, places, factors, own, (a_first, b_first, near_a_first, near_b_first), weights
    )
    near_a_last = replica_swap(a_last, 1)
    near_b_last = replica_swap(b_last, 1)
    moved_last = replica_swap(a_last, 2)
    third, third_partner = first_planes(2, places, factors, own, (a_last, b_last), weights)
    spectral, last_partner = spectrum(
        3, places, factors, own, (head, third), (near_a_last, near_b_last), kernel, weights
    )
    partners = partner, third_partner, last_partner
    sent = exchange_terms((FAR_SENT, NEAR_SENT), slab_rows, places, spectral, partners, weights)
    met_far = replica_swap(sent[0], 1)
    met_near = replica_swap(sent[1], 1)
    kept = exchange_terms((FAR_KEPT, NEAR_KEPT), slab_rows, places, spectral, partners, weights)
    arrived = replica_swap(blend(factors, kept[0], met_far), 2)
    row = gram(
        places,
        factors,
        (kept[0], met_far),
        (kept[1], met_near),
        own,
        a_first,
        near_b_first,
        moved_first,
        a_last,
        near_b_last,
        moved_last,
    )
    near_sum = blend(factors, kept[1], met_near)
    row = row + replica_swap(row, 1)
    other = replica_swap(row, 2)
    exchanged, margin = finish(near_sum, arrived, row, other, blocks)
    return exchanged.reshape(1, cells // replicas), margin


def local(orbitals, offsets):
    blocks, replicas = lax.axis_size("blk"), lax.axis_size("rep")
    table = cas_table(NG)
    forward = table.reshape(NG, NG // 2, 2).transpose(0, 2, 1).reshape(NG, NG)
    paired = jnp.kron(jnp.eye(2, dtype=jnp.float32), table)
    tables = forward, forward.T, paired
    if is_folded(blocks, replicas):
        return folded(orbitals, offsets, tables)
    return stepped(orbitals, offsets, tables)


def is_folded(blocks, replicas):
    return blocks == replicas == len(MET)


def solution(mesh):
    placed = (P(("groups", "blk"), None), P("groups"))
    step = jax.shard_map(
        local,
        mesh=mesh,
        in_specs=placed,
        out_specs=(P(("groups", "blk"), "rep"), P(("groups", "blk"), None)),
        check_vma=False,
    )
    if not is_folded(mesh.shape["blk"], mesh.shape["rep"]):
        return step
    return step
```

```python
import functools

import jax
import jax.numpy as jnp
from jax import lax
from jax.experimental import pallas as pl
from jax.experimental.pallas import tpu as pltpu
from jax.sharding import PartitionSpec as P


NG = 64
STEPS = 3
LANES = 128
HALF = LANES // 2
PITCH = NG + 1
GROUP = 256
MET = (3, 1, 2, 0)
SENT = (3, 1, 2, 1)
SENT_A = (3, 3, 2, 2)
SENT_B = (1, 1, 1, 1)
SLABS = len(MET)
SAME, LOW, HIGH, FAR_SENT, NEAR_SENT, FAR_KEPT, NEAR_KEPT, OWN, OTHERS = 0, 1, 2, 3, 4, 5, 6, 7, 9
screen_scale = 0.05


def passed_along(block, axis, distance):
    devices = range(lax.axis_size(axis))
    route = [((i - distance) % len(devices), i) for i in devices]
    return lax.ppermute(block, axis, route)


def cas_table(grid_points):
    grid_index = jnp.arange(grid_points, dtype=jnp.int32)
    product = grid_index[:, None] * grid_index[None, :] % grid_points
    phase_angle = 2.0 * jnp.pi / grid_points * product.astype(jnp.float32)
    return jnp.cos(phase_angle) + jnp.sin(phase_angle)


def screened_kernel(grid_points):
    def squares(index):
        folded = jnp.where(index <= grid_points // 2, index, index - grid_points).astype(jnp.float32)
        return folded * folded

    shape = (grid_points * grid_points // 2, 2 * grid_points)
    row = lax.broadcasted_iota(jnp.int32, shape, 0)
    lane = lax.broadcasted_iota(jnp.int32, shape, 1)
    k_squared = (
        squares(row % grid_points)
        + squares(2 * (row // grid_points) + lane // grid_points)
        + squares(lane % grid_points)
    )
    safe_square = jnp.maximum(k_squared, 1.0)
    screened = (
        4.0
        * jnp.pi
        / (screen_scale * safe_square)
        * (1.0 - jnp.exp(-screen_scale * safe_square / (4.0 * jnp.pi)))
    )
    return jnp.where(k_squared > 0.5, screened, jnp.ones_like(screened))


def high_low(value):
    high = value.astype(jnp.bfloat16)
    return high, (value - high.astype(jnp.float32)).astype(jnp.bfloat16)


def dot(a, b):
    return lax.dot_general(a, b, (((1,), (0,)), ((), ())), preferred_element_type=jnp.float32)


def swapped(first, second, low_half):
    return (
        jnp.where(low_half, first, pltpu.roll(second, HALF, 1)),
        jnp.where(low_half, pltpu.roll(first, HALF, 1), second),
    )


def left_weights(table):
    high, low = high_low(table)
    return jnp.concatenate([high, high, low], axis=1)


def lane_weights(table):
    high, low = high_low(table)
    return jnp.concatenate(
        [jnp.concatenate([high, low], axis=1), jnp.concatenate([high, jnp.zeros_like(low)], axis=1)],
        axis=0,
    )


def from_left(weights, value):
    high, low = high_low(value)
    return dot(weights, jnp.concatenate([high, low, high], axis=0))


def along_lanes(value, weights):
    high, low = high_low(value)
    both = dot(jnp.concatenate([high, low], axis=1), weights)
    return both[:, :LANES] + both[:, LANES:]


def low_mask(rows):
    return lax.broadcasted_iota(jnp.int32, (rows, LANES), 1) < HALF


def kernel_call(body, shape, spaces, flops, cells, **more):
    memory = {"s": pltpu.SMEM, "v": pltpu.VMEM}
    return pl.pallas_call(
        body,
        out_shape=jax.ShapeDtypeStruct(shape, jnp.float32),
        in_specs=[pl.BlockSpec(memory_space=memory[space]) for space in spaces],
        out_specs=pl.BlockSpec(memory_space=pltpu.VMEM),
        compiler_params=pltpu.CompilerParams(vmem_limit_bytes=24 << 20),
        cost_estimate=pl.CostEstimate(flops=flops, bytes_accessed=4 * cells, transcendentals=0),
        **more,
    )


def weights_body(forward, backward, paired, left_y, left_back, lanes):
    left_y[...] = left_weights(forward[...])
    left_back[...] = left_weights(backward[...])
    lanes[...] = lane_weights(paired[...])


def prepared_weights(forward, backward, paired):
    vmem = pl.BlockSpec(memory_space=pltpu.VMEM)
    shapes = (NG, 3 * NG), (NG, 3 * NG), (2 * LANES, 2 * LANES)
    return pl.pallas_call(
        weights_body,
        out_shape=[jax.ShapeDtypeStruct(shape, jnp.bfloat16) for shape in shapes],
        in_specs=[vmem] * 3,
        out_specs=[vmem] * 3,
        name="weights",
    )(forward, backward, paired)


def planes_body(own, visit_at, alone, left_y, lanes, along_z, out, *, first_row):
    plane = NG // 2
    mask = low_mask(plane)
    w_forward = left_y[...]
    w_lanes = lanes[...]
    rows = along_z.shape[0]
    for at in range(0, rows, GROUP):
        mine = own[first_row + at : first_row + at + GROUP, :]
        density = mine * jnp.where(alone, mine, visit_at(at))
        along_z[at : at + GROUP, :] = along_lanes(density, w_lanes)

    def step_planes(step, _):
        at = step * (4 * plane)
        blocks = []
        for half in range(2):
            base = at + half * 2 * plane
            lines = [along_z[pl.ds(pl.multiple_of(base + odd * plane, plane), plane), :] for odd in range(2)]
            blocks.append(jnp.concatenate(swapped(*lines, mask), axis=0))
        along_y = from_left(w_forward, jnp.concatenate(blocks, axis=1))
        out[pl.ds(step * (2 * PITCH), NG), :] = along_y[:, :LANES]
        out[pl.ds(step * (2 * PITCH) + PITCH, NG), :] = along_y[:, LANES:]
        return 0

    steps = rows // (4 * plane)
    lax.fori_loop(0, steps, step_planes, 0, unroll=steps)


def slabs_body(places, own, choices, left_y, lanes, along_z, out, partner, *, first_slab):
    slab_rows = choices[0].shape[0]
    even = places[LOW] == 0
    alone = places[SAME] == 1
    first_row = first_slab * slab_rows

    def visit_at(at):
        inside = slice(at % slab_rows, at % slab_rows + GROUP)
        index = at // slab_rows * 2
        value = jnp.where(even, choices[index][inside, :], choices[index + 1][inside, :])
        partner[at : at + GROUP, :] = jnp.where(alone, own[first_row + at : first_row + at + GROUP, :], value)
        return value

    planes_body(own, visit_at, alone, left_y, lanes, along_z, out, first_row=first_row)


def first_body(places, factors, own, *refs, first_slab, count):
    choices, (left_y, lanes, out, partner, along_z) = refs[: 2 * count], refs[2 * count :]
    slabs_body(places, own, choices, left_y, lanes, along_z, out, partner, first_slab=first_slab)


def spectrum_body(places, factors, own, *refs, heads, first_slab, count, which):
    parts, known, rest = refs[:heads], refs[heads : 2 * heads], refs[2 * heads :]
    choices, rest = rest[: 2 * count], rest[2 * count :]
    kernel, left_y, left_back, lanes, out, partner, *outs, tail, along_z, back_y = rest
    plane = NG // 2
    mask = low_mask(plane)
    slabs_body(places, own, choices, left_y, lanes, along_z, tail, partner, first_slab=first_slab)
    parts = (*parts, tail)
    w_forward = left_y[...]
    w_backward = left_back[...]

    def columns(step, _):
        blocks = []
        for part in range(2):
            row = 4 * step + 2 * part
            first, second = (
                jnp.concatenate(
                    [ref[pl.ds(row + odd, ref.shape[0] // PITCH, stride=PITCH), :] for ref in parts], axis=0
                )
                for odd in range(2)
            )
            blocks.append(jnp.concatenate(swapped(first, second, mask), axis=0))
        along_x = from_left(w_forward, jnp.concatenate(blocks, axis=1))
        at = pl.multiple_of(step * (2 * NG), 2 * NG)
        weight = jnp.concatenate([kernel[pl.ds(at, NG), :], kernel[pl.ds(at + NG, NG), :]], axis=1)
        returned = from_left(w_backward, along_x * weight)
        for part in range(2):
            block = returned[:, part * LANES : (part + 1) * LANES]
            row = 4 * step + 2 * part
            for odd, value in enumerate(swapped(block[:plane], block[plane:], mask)):
                out[pl.ds(row + odd, plane, stride=PITCH), :] = value
        return 0

    lax.fori_loop(0, NG // 4, columns, 0, unroll=NG // 4)
    fill_terms(places, out, (*known, partner), left_back, lanes, outs, back_y, which)


def planes_call(body, spaces, out_rows, scratch_rows, flops, cells):
    smem = pl.BlockSpec(memory_space=pltpu.SMEM)
    vmem = pl.BlockSpec(memory_space=pltpu.VMEM)
    return pl.pallas_call(
        body,
        out_shape=[jax.ShapeDtypeStruct((rows, LANES), jnp.float32) for rows in out_rows],
        in_specs=[smem] * 2 + [vmem] * spaces,
        out_specs=[vmem] * len(out_rows),
        scratch_shapes=[pltpu.VMEM((rows, LANES), jnp.float32) for rows in scratch_rows],
        compiler_params=pltpu.CompilerParams(vmem_limit_bytes=24 << 20),
        cost_estimate=pl.CostEstimate(flops=flops, bytes_accessed=4 * cells, transcendentals=0),
    )


def first_planes(first_slab, places, factors, own, choices, weights):
    left_y, _, lanes = weights
    count = len(choices) // 2
    rows = count * choices[0].shape[0]
    body = functools.partial(first_body, first_slab=first_slab, count=count)
    pitched = rows // NG * PITCH
    return planes_call(
        body, 3 + 2 * count, (pitched, rows), (rows,), rows * LANES * NG * 4, 4 * rows * LANES
    )(places, factors, own, *choices, left_y, lanes)


def spectrum(first_slab, which, places, factors, own, heads, known, choices, kernel, weights):
    count = len(choices) // 2
    rows, slab_rows = own.shape[0], choices[0].shape[0]
    last = count * slab_rows
    body = functools.partial(spectrum_body, heads=len(heads), first_slab=first_slab, count=count, which=which)
    return planes_call(
        body,
        5 + 2 * len(heads) + 2 * count,
        (rows // NG * PITCH, last) + (slab_rows,) * len(which),
        (last // NG * PITCH, last, len(which) * slab_rows),
        rows * LANES * NG * 16,
        8 * rows * LANES,
    )(places, factors, own, *heads, *known, *choices, kernel, *weights)


def terms_body(places, spectral, *refs, which):
    partners, (left_back, lanes, *outs, back_y) = refs[: -3 - len(which)], refs[-3 - len(which) :]
    fill_terms(places, spectral, partners, left_back, lanes, outs, back_y, which)


def fill_terms(places, spectral, partners, left_back, lanes, outs, back_y, which):
    plane = NG // 2
    mask = low_mask(plane)
    w_backward = left_back[...]
    w_lanes = lanes[...]
    slab_rows = outs[0].shape[0]
    steps = slab_rows // (4 * plane)

    def partner_at(slab, at):
        value, first_slab = None, 0
        for piece in partners:
            count = piece.shape[0] // slab_rows
            row = jnp.clip(slab - first_slab, 0, count - 1) * slab_rows + at
            here = piece[pl.ds(pl.multiple_of(row, 8), GROUP), :]
            value = here if value is None else jnp.where(slab >= first_slab, here, value)
            first_slab += count
        return value

    for index, entry in enumerate(which):
        start = places[entry] * slab_rows
        for step in range(steps):
            row = (start // NG + 2 * step) * PITCH
            pair = jnp.concatenate([spectral[pl.ds(row, NG), :], spectral[pl.ds(row + PITCH, NG), :]], axis=1)
            along_y = from_left(w_backward, pair)
            for half in range(2):
                block = along_y[:, half * LANES : (half + 1) * LANES]
                for second, value in enumerate(swapped(block[:plane], block[plane:], mask)):
                    line = index * slab_rows + (4 * step + 2 * half + second) * plane
                    back_y[line : line + plane, :] = value
    for index, entry in enumerate(which):
        for at in range(0, slab_rows, GROUP):
            line = index * slab_rows + at
            potential = along_lanes(back_y[line : line + GROUP, :], w_lanes)
            outs[index][at : at + GROUP, :] = potential * (partner_at(places[entry], at) * (1.0 / NG**3))


def exchange_terms(which, slab_rows, places, spectral, partners, weights):
    cells = len(which) * slab_rows * LANES
    vmem = pl.BlockSpec(memory_space=pltpu.VMEM)
    return pl.pallas_call(
        functools.partial(terms_body, which=which),
        out_shape=[jax.ShapeDtypeStruct((slab_rows, LANES), jnp.float32) for _ in which],
        in_specs=[pl.BlockSpec(memory_space=pltpu.SMEM)] + [vmem] * (3 + len(partners)),
        out_specs=[vmem] * len(which),
        scratch_shapes=[pltpu.VMEM((len(which) * slab_rows, LANES), jnp.float32)],
        compiler_params=pltpu.CompilerParams(vmem_limit_bytes=24 << 20),
        cost_estimate=pl.CostEstimate(flops=cells * NG * 12, bytes_accessed=16 * cells, transcendentals=0),
        name="terms",
    )(places, spectral, *partners, weights[1], weights[2])


def blend_body(factors, kept, met, out):
    out[...] = factors[0] * kept[...] + factors[1] * met[...]


def blend(factors, kept, met):
    return kernel_call(blend_body, kept.shape, "svv", 3 * kept.size, 3 * kept.size)(factors, kept, met)


def finish_body(near_sum, arrived, row, other, exchanged, margin):
    exchanged[...] = near_sum[...] + arrived[...]
    margin[...] = (row[...] + other[...])[:1, : margin.shape[1]]


def finish(near_sum, arrived, row, other, columns):
    vmem = pl.BlockSpec(memory_space=pltpu.VMEM)
    return pl.pallas_call(
        finish_body,
        out_shape=[
            jax.ShapeDtypeStruct(near_sum.shape, jnp.float32),
            jax.ShapeDtypeStruct((1, columns), jnp.float32),
        ],
        in_specs=[vmem] * 4,
        out_specs=[vmem] * 2,
        compiler_params=pltpu.CompilerParams(vmem_limit_bytes=24 << 20),
        cost_estimate=pl.CostEstimate(
            flops=near_sum.size, bytes_accessed=12 * near_sum.size, transcendentals=0
        ),
        name="finish",
    )(near_sum, arrived, row, other)


def seat_body(offsets, places, factors, *, blocks, replicas):
    block, replica = lax.axis_index("blk"), lax.axis_index("rep")
    low, high = replica % 2, replica // 2

    def listed(numbers, index):
        value = jnp.int32(numbers[0])
        for other in range(1, len(numbers)):
            value = jnp.where(index == other, jnp.int32(numbers[other]), value)
        return value

    partners = [block ^ listed(MET, replica), block ^ listed(MET, replica ^ 1)]
    others = [
        block,
        block ^ listed(SENT, replica),
        block ^ listed(SENT, replica ^ 1),
        block ^ listed(SENT, (replica ^ 2) // 2 * 2),
    ]
    far, near = 2 * (1 - high), 2 * high
    same = (listed(MET, replica) == 0).astype(jnp.int32)
    slabs = [far + 1 - low, near + 1 - low, far + low, near + low, low, 2 + low]
    for index, value in enumerate([same, low, high] + slabs + others):
        places[index] = value.astype(jnp.int32)
    shifts = [(offsets[r] + step) % blocks for r in range(replicas) for step in range(STEPS)]
    apart = [(block - partner, 1.0) for partner in partners]
    apart += [(other - partner, 1.0 / NG**3) for partner in partners for other in others]
    for index, (distance, scale) in enumerate(apart):
        wanted = (distance + blocks) % blocks
        hits = jnp.int32(0)
        for shift in shifts:
            hits += (shift == wanted).astype(jnp.int32)
        factors[index] = hits.astype(jnp.float32) * scale


def seat(offsets, blocks, replicas):
    smem = pl.BlockSpec(memory_space=pltpu.SMEM)
    return pl.pallas_call(
        functools.partial(seat_body, blocks=blocks, replicas=replicas),
        out_shape=[
            jax.ShapeDtypeStruct((OTHERS + 4,), jnp.int32),
            jax.ShapeDtypeStruct((10,), jnp.float32),
        ],
        in_specs=[smem],
        out_specs=[smem] * 2,
        name="seat",
    )(offsets)


def gram_body(places, factors, far, met_far, near, met_near, own, *refs):
    *stores, out = refs
    even = places[LOW] == 0
    rows = far.shape[0]
    chunk = 64

    def folded_rows(value):
        return jnp.sum(value.reshape(chunk // 8, 8, LANES), axis=0)

    totals = (jnp.zeros((8, LANES), jnp.float32),) * 8
    for side in range(2):
        is_near = places[HIGH] == side
        piece_a, near_b, moved_a = stores[3 * side : 3 * side + 3]
        own_row = places[OWN + side] * rows

        def step(index, totals, is_near=is_near, piece_a=piece_a, near_b=near_b, moved_a=moved_a, own_row=own_row):
            inside = index * chunk
            at = pl.ds(pl.multiple_of(inside, chunk), chunk)
            mine = pl.ds(pl.multiple_of(own_row + inside, chunk), chunk)
            terms = (
                jnp.where(is_near, near[at, :], far[at, :]),
                jnp.where(is_near, met_near[at, :], met_far[at, :]),
            )
            of_a, of_b = piece_a[at, :], near_b[at, :]
            orbitals = (own[mine, :], jnp.where(even, of_a, of_b), jnp.where(even, of_b, of_a), moved_a[at, :])
            return tuple(
                totals[4 * t + o] + folded_rows(terms[t] * orbitals[o]) for t in range(2) for o in range(4)
            )

        totals = lax.fori_loop(0, rows // chunk, step, totals, unroll=4)
    lane = lax.broadcasted_iota(jnp.int32, (8, LANES), 1)
    result = jnp.zeros((8, LANES), jnp.float32)
    for o in range(4):
        value = jnp.sum(factors[2 + o] * totals[o] + factors[6 + o] * totals[4 + o], axis=(0, 1), keepdims=True)
        result = jnp.where(lane == places[OTHERS + o], value, result)
    out[...] = result


def gram(places, factors, far, near, own, *stores):
    cells = far[0].size
    return kernel_call(
        gram_body, (8, LANES), "ssvvvvv" + "v" * len(stores), 32 * cells, 12 * cells
    )(places, factors, *far, *near, own, *stores)


def position_block(orbital_block, amount):
    bit_count = (lax.axis_size("blk") - 1).bit_length()
    for bit_level in range(bit_count):
        moved_block = passed_along(orbital_block, "blk", 1 << bit_level)
        orbital_block = jnp.where(amount // (1 << bit_level) % 2 == 1, moved_block, orbital_block)
    return orbital_block


def stepped(orbitals, offsets, tables):
    blocks, replicas = lax.axis_size("blk"), lax.axis_size("rep")
    replica = lax.axis_index("rep")
    cells = orbitals.shape[1]
    rows = cells // LANES
    weights = prepared_weights(*tables)
    kernel = screened_kernel(NG)
    first = position_block(orbitals, (offsets[replica] + STEPS // 2) % blocks)
    visits = [first]
    for distance in range(1, STEPS // 2 + 1):
        visits.append(passed_along(first, "blk", -distance))
        visits.append(passed_along(first, "blk", distance))
    own = orbitals.reshape(rows, LANES)
    places = jnp.zeros((OTHERS,), jnp.int32)
    factors = jnp.zeros((2,), jnp.float32)
    whole = jnp.zeros((rows, LANES), jnp.float32)
    for visit in visits:
        visit = visit.reshape(rows, LANES)
        slab_rows = rows // SLABS
        slabs = [visit[slab * slab_rows : (slab + 1) * slab_rows] for slab in range(SLABS)]
        choices = [slabs[index // 2] for index in range(2 * SLABS)]
        head, partner_a = first_planes(0, places, factors, own, choices[:4], weights)
        numbers = jnp.arange(SLABS, dtype=jnp.int32)
        spots = places.at[FAR_SENT : FAR_SENT + SLABS].set(numbers)
        which = tuple(range(FAR_SENT, FAR_SENT + SLABS))
        _, _, *terms = spectrum(
            2, which, spots, factors, own, (head,), (partner_a,), choices[4:], kernel, weights
        )
        whole = whole + jnp.concatenate(terms, axis=0)
    exchanged = lax.psum_scatter(whole.reshape(1, cells), "rep", scatter_dimension=1, tiled=True)
    quarter = lax.dynamic_slice_in_dim(orbitals, replica * (cells // replicas), cells // replicas, 1)
    slab_orbitals = lax.all_to_all(quarter, "blk", split_axis=1, concat_axis=0, tiled=True)
    slab_exchanged = lax.all_to_all(exchanged, "blk", split_axis=1, concat_axis=0, tiled=True)
    partial_value = lax.dot_general(
        slab_orbitals, slab_exchanged, (((1,), (1,)), ((), ())), precision=lax.Precision.HIGHEST
    ) / float(NG**3)
    gram_rows = lax.psum_scatter(partial_value, "blk", scatter_dimension=0, tiled=True)
    return exchanged, lax.psum(gram_rows, "rep")


def folded(orbitals, offsets, tables):
    blocks, replicas = lax.axis_size("blk"), lax.axis_size("rep")
    replica = lax.axis_index("rep")
    cells = orbitals.shape[1]
    rows = cells // LANES
    slab_rows = rows // replicas
    weights = prepared_weights(*tables)
    own = orbitals.reshape(rows, LANES)
    low = replica % 2
    places, factors = seat(offsets, blocks, replicas)

    def along_blocks(value, sent):
        route = [((b ^ sent[r]) * replicas + r, b * replicas + r) for b in range(blocks) for r in range(replicas)]
        return lax.ppermute(value, ("blk", "rep"), route)

    def replica_swap(value, bit):
        return lax.ppermute(value, "rep", [(r, r ^ bit) for r in range(replicas)])

    def slab_of(index):
        return lax.dynamic_slice_in_dim(own, index * slab_rows, slab_rows, 0)

    a_first = along_blocks(slab_of(low), SENT_A)
    b_first = along_blocks(slab_of(1 - low), SENT_B)
    b_last = along_blocks(slab_of(3 - low), SENT_B)
    a_last = along_blocks(slab_of(2 + low), SENT_A)
    kernel = screened_kernel(NG)

    near_a_first = replica_swap(a_first, 1)
    near_b_first = replica_swap(b_first, 1)
    moved_first = replica_swap(a_first, 2)
    head, partner = first_planes(
        0, places, factors, own, (a_first, b_first, near_a_first, near_b_first), weights
    )
    near_a_last = replica_swap(a_last, 1)
    near_b_last = replica_swap(b_last, 1)
    moved_last = replica_swap(a_last, 2)
    third, third_partner = first_planes(2, places, factors, own, (a_last, b_last), weights)
    spectral, last_partner, *sent = spectrum(
        3,
        (FAR_SENT, NEAR_SENT),
        places,
        factors,
        own,
        (head, third),
        (partner, third_partner),
        (near_a_last, near_b_last),
        kernel,
        weights,
    )
    partners = partner, third_partner, last_partner
    met_far = replica_swap(sent[0], 1)
    met_near = replica_swap(sent[1], 1)
    kept = exchange_terms((FAR_KEPT, NEAR_KEPT), slab_rows, places, spectral, partners, weights)
    arrived = replica_swap(blend(factors, kept[0], met_far), 2)
    row = gram(
        places,
        factors,
        (kept[0], met_far),
        (kept[1], met_near),
        own,
        a_first,
        near_b_first,
        moved_first,
        a_last,
        near_b_last,
        moved_last,
    )
    near_sum = blend(factors, kept[1], met_near)
    row = row + replica_swap(row, 1)
    other = replica_swap(row, 2)
    exchanged, margin = finish(near_sum, arrived, row, other, blocks)
    return exchanged.reshape(1, cells // replicas), margin


def local(orbitals, offsets):
    blocks, replicas = lax.axis_size("blk"), lax.axis_size("rep")
    table = cas_table(NG)
    forward = table.reshape(NG, NG // 2, 2).transpose(0, 2, 1).reshape(NG, NG)
    paired = jnp.kron(jnp.eye(2, dtype=jnp.float32), table)
    tables = forward, forward.T, paired
    if is_folded(blocks, replicas):
        return folded(orbitals, offsets, tables)
    return stepped(orbitals, offsets, tables)


def is_folded(blocks, replicas):
    return blocks == replicas == len(MET)


def solution(mesh):
    placed = (P(("groups", "blk"), None), P("groups"))
    step = jax.shard_map(
        local,
        mesh=mesh,
        in_specs=placed,
        out_specs=(P(("groups", "blk"), "rep"), P(("groups", "blk"), None)),
        check_vma=False,
    )
    if not is_folded(mesh.shape["blk"], mesh.shape["rep"]):
        return step
    return step
```

```python
import functools

import jax
import jax.numpy as jnp
from jax import lax
from jax.experimental import pallas as pl
from jax.experimental.pallas import tpu as pltpu
from jax.sharding import PartitionSpec as P


NG = 64
STEPS = 3
LANES = 128
HALF = LANES // 2
PITCH = NG + 1
GROUP = 256
MET = (3, 1, 2, 0)
SENT = (3, 1, 2, 1)
SENT_A = (3, 3, 2, 2)
SENT_B = (1, 1, 1, 1)
SLABS = len(MET)
SAME, LOW, HIGH, FAR_SENT, NEAR_SENT, FAR_KEPT, NEAR_KEPT, OWN, OTHERS = 0, 1, 2, 3, 4, 5, 6, 7, 9
screen_scale = 0.05


def passed_along(block, axis, distance):
    devices = range(lax.axis_size(axis))
    route = [((i - distance) % len(devices), i) for i in devices]
    return lax.ppermute(block, axis, route)


def cas_table(grid_points):
    grid_index = jnp.arange(grid_points, dtype=jnp.int32)
    product = grid_index[:, None] * grid_index[None, :] % grid_points
    phase_angle = 2.0 * jnp.pi / grid_points * product.astype(jnp.float32)
    return jnp.cos(phase_angle) + jnp.sin(phase_angle)


def screened_kernel(grid_points):
    def squares(index):
        folded = jnp.where(index <= grid_points // 2, index, index - grid_points).astype(jnp.float32)
        return folded * folded

    shape = (grid_points * grid_points // 2, 2 * grid_points)
    row = lax.broadcasted_iota(jnp.int32, shape, 0)
    lane = lax.broadcasted_iota(jnp.int32, shape, 1)
    k_squared = (
        squares(row % grid_points)
        + squares(2 * (row // grid_points) + lane // grid_points)
        + squares(lane % grid_points)
    )
    safe_square = jnp.maximum(k_squared, 1.0)
    screened = (
        4.0
        * jnp.pi
        / (screen_scale * safe_square)
        * (1.0 - jnp.exp(-screen_scale * safe_square / (4.0 * jnp.pi)))
    )
    return jnp.where(k_squared > 0.5, screened, jnp.ones_like(screened))


def high_low(value):
    high = value.astype(jnp.bfloat16)
    return high, (value - high.astype(jnp.float32)).astype(jnp.bfloat16)


def dot(a, b):
    return lax.dot_general(a, b, (((1,), (0,)), ((), ())), preferred_element_type=jnp.float32)


def swapped(first, second, low_half):
    return (
        jnp.where(low_half, first, pltpu.roll(second, HALF, 1)),
        jnp.where(low_half, pltpu.roll(first, HALF, 1), second),
    )


def left_weights(table):
    high, low = high_low(table)
    return jnp.concatenate([high, high, low], axis=1)


def lane_weights(table):
    high, low = high_low(table)
    return jnp.concatenate(
        [jnp.concatenate([high, low], axis=1), jnp.concatenate([high, jnp.zeros_like(low)], axis=1)],
        axis=0,
    )


def from_left(weights, value):
    high, low = high_low(value)
    return dot(weights, jnp.concatenate([high, low, high], axis=0))


def along_lanes(value, weights):
    high, low = high_low(value)
    both = dot(jnp.concatenate([high, low], axis=1), weights)
    return both[:, :LANES] + both[:, LANES:]


def low_mask(rows):
    return lax.broadcasted_iota(jnp.int32, (rows, LANES), 1) < HALF


def kernel_call(body, shape, spaces, flops, cells, **more):
    memory = {"s": pltpu.SMEM, "v": pltpu.VMEM}
    return pl.pallas_call(
        body,
        out_shape=jax.ShapeDtypeStruct(shape, jnp.float32),
        in_specs=[pl.BlockSpec(memory_space=memory[space]) for space in spaces],
        out_specs=pl.BlockSpec(memory_space=pltpu.VMEM),
        compiler_params=pltpu.CompilerParams(vmem_limit_bytes=24 << 20),
        cost_estimate=pl.CostEstimate(flops=flops, bytes_accessed=4 * cells, transcendentals=0),
        **more,
    )


def weights_body(forward, backward, paired, left_y, left_back, lanes):
    left_y[...] = left_weights(forward[...])
    left_back[...] = left_weights(backward[...])
    lanes[...] = lane_weights(paired[...])


def prepared_weights(forward, backward, paired):
    vmem = pl.BlockSpec(memory_space=pltpu.VMEM)
    shapes = (NG, 3 * NG), (NG, 3 * NG), (2 * LANES, 2 * LANES)
    return pl.pallas_call(
        weights_body,
        out_shape=[jax.ShapeDtypeStruct(shape, jnp.bfloat16) for shape in shapes],
        in_specs=[vmem] * 3,
        out_specs=[vmem] * 3,
        name="weights",
    )(forward, backward, paired)


def planes_body(own, visit_at, alone, left_y, lanes, along_z, out, *, first_row):
    plane = NG // 2
    mask = low_mask(plane)
    w_forward = left_y[...]
    w_lanes = lanes[...]
    rows = along_z.shape[0]
    for at in range(0, rows, GROUP):
        mine = own[first_row + at : first_row + at + GROUP, :]
        density = mine * jnp.where(alone, mine, visit_at(at))
        along_z[at : at + GROUP, :] = along_lanes(density, w_lanes)

    def step_planes(step, _):
        at = step * (4 * plane)
        blocks = []
        for half in range(2):
            base = at + half * 2 * plane
            lines = [along_z[pl.ds(pl.multiple_of(base + odd * plane, plane), plane), :] for odd in range(2)]
            blocks.append(jnp.concatenate(swapped(*lines, mask), axis=0))
        along_y = from_left(w_forward, jnp.concatenate(blocks, axis=1))
        out[pl.ds(step * (2 * PITCH), NG), :] = along_y[:, :LANES]
        out[pl.ds(step * (2 * PITCH) + PITCH, NG), :] = along_y[:, LANES:]
        return 0

    steps = rows // (4 * plane)
    lax.fori_loop(0, steps, step_planes, 0, unroll=steps)


def slabs_body(places, own, choices, left_y, lanes, along_z, out, partner, *, first_slab):
    slab_rows = choices[0].shape[0]
    even = places[LOW] == 0
    alone = places[SAME] == 1
    first_row = first_slab * slab_rows

    def visit_at(at):
        inside = slice(at % slab_rows, at % slab_rows + GROUP)
        index = at // slab_rows * 2
        value = jnp.where(even, choices[index][inside, :], choices[index + 1][inside, :])
        partner[at : at + GROUP, :] = jnp.where(alone, own[first_row + at : first_row + at + GROUP, :], value)
        return value

    planes_body(own, visit_at, alone, left_y, lanes, along_z, out, first_row=first_row)


def first_body(places, factors, own, *refs, first_slab, count):
    choices, (left_y, lanes, out, partner, along_z) = refs[: 2 * count], refs[2 * count :]
    slabs_body(places, own, choices, left_y, lanes, along_z, out, partner, first_slab=first_slab)


def spectrum_body(places, factors, own, *refs, heads, first_slab, count, which):
    parts, known, rest = refs[:heads], refs[heads : 2 * heads], refs[2 * heads :]
    choices, rest = rest[: 2 * count], rest[2 * count :]
    kernel, left_y, left_back, lanes, out, partner, *outs, tail, along_z, back_y = rest
    plane = NG // 2
    mask = low_mask(plane)
    slabs_body(places, own, choices, left_y, lanes, along_z, tail, partner, first_slab=first_slab)
    parts = (*parts, tail)
    w_forward = left_y[...]
    w_backward = left_back[...]

    def columns(step, _):
        blocks = []
        for part in range(2):
            row = 4 * step + 2 * part
            first, second = (
                jnp.concatenate(
                    [ref[pl.ds(row + odd, ref.shape[0] // PITCH, stride=PITCH), :] for ref in parts], axis=0
                )
                for odd in range(2)
            )
            blocks.append(jnp.concatenate(swapped(first, second, mask), axis=0))
        along_x = from_left(w_forward, jnp.concatenate(blocks, axis=1))
        at = pl.multiple_of(step * (2 * NG), 2 * NG)
        weight = jnp.concatenate([kernel[pl.ds(at, NG), :], kernel[pl.ds(at + NG, NG), :]], axis=1)
        returned = from_left(w_backward, along_x * weight)
        for part in range(2):
            block = returned[:, part * LANES : (part + 1) * LANES]
            row = 4 * step + 2 * part
            for odd, value in enumerate(swapped(block[:plane], block[plane:], mask)):
                out[pl.ds(row + odd, plane, stride=PITCH), :] = value
        return 0

    lax.fori_loop(0, NG // 4, columns, 0, unroll=NG // 4)
    fill_terms(places, out, (*known, partner), left_back, lanes, outs, back_y, which)


def planes_call(body, spaces, out_rows, scratch_rows, flops, cells):
    smem = pl.BlockSpec(memory_space=pltpu.SMEM)
    vmem = pl.BlockSpec(memory_space=pltpu.VMEM)
    return pl.pallas_call(
        body,
        out_shape=[jax.ShapeDtypeStruct((rows, LANES), jnp.float32) for rows in out_rows],
        in_specs=[smem] * 2 + [vmem] * spaces,
        out_specs=[vmem] * len(out_rows),
        scratch_shapes=[pltpu.VMEM((rows, LANES), jnp.float32) for rows in scratch_rows],
        compiler_params=pltpu.CompilerParams(vmem_limit_bytes=24 << 20),
        cost_estimate=pl.CostEstimate(flops=flops, bytes_accessed=4 * cells, transcendentals=0),
    )


def first_planes(first_slab, places, factors, own, choices, weights):
    left_y, _, lanes = weights
    count = len(choices) // 2
    rows = count * choices[0].shape[0]
    body = functools.partial(first_body, first_slab=first_slab, count=count)
    pitched = rows // NG * PITCH
    return planes_call(
        body, 3 + 2 * count, (pitched, rows), (rows,), rows * LANES * NG * 4, 4 * rows * LANES
    )(places, factors, own, *choices, left_y, lanes)


def spectrum(first_slab, which, places, factors, own, heads, known, choices, kernel, weights):
    count = len(choices) // 2
    rows, slab_rows = own.shape[0], choices[0].shape[0]
    last = count * slab_rows
    body = functools.partial(spectrum_body, heads=len(heads), first_slab=first_slab, count=count, which=which)
    return planes_call(
        body,
        5 + 2 * len(heads) + 2 * count,
        (rows // NG * PITCH, last) + (slab_rows,) * len(which),
        (last // NG * PITCH, last, len(which) * slab_rows),
        rows * LANES * NG * 16,
        8 * rows * LANES,
    )(places, factors, own, *heads, *known, *choices, kernel, *weights)


def terms_body(places, spectral, *refs, which):
    partners, (left_back, lanes, *outs, back_y) = refs[: -3 - len(which)], refs[-3 - len(which) :]
    fill_terms(places, spectral, partners, left_back, lanes, outs, back_y, which)


def fill_terms(places, spectral, partners, left_back, lanes, outs, back_y, which):
    plane = NG // 2
    mask = low_mask(plane)
    w_backward = left_back[...]
    w_lanes = lanes[...]
    slab_rows = outs[0].shape[0]
    steps = slab_rows // (4 * plane)

    def partner_at(slab, at):
        value, first_slab = None, 0
        for piece in partners:
            count = piece.shape[0] // slab_rows
            row = jnp.clip(slab - first_slab, 0, count - 1) * slab_rows + at
            here = piece[pl.ds(pl.multiple_of(row, 8), GROUP), :]
            value = here if value is None else jnp.where(slab >= first_slab, here, value)
            first_slab += count
        return value

    for index, entry in enumerate(which):
        start = places[entry] * slab_rows
        for step in range(steps):
            row = (start // NG + 2 * step) * PITCH
            pair = jnp.concatenate([spectral[pl.ds(row, NG), :], spectral[pl.ds(row + PITCH, NG), :]], axis=1)
            along_y = from_left(w_backward, pair)
            for half in range(2):
                block = along_y[:, half * LANES : (half + 1) * LANES]
                for second, value in enumerate(swapped(block[:plane], block[plane:], mask)):
                    line = index * slab_rows + (4 * step + 2 * half + second) * plane
                    back_y[line : line + plane, :] = value
    for index, entry in enumerate(which):
        for at in range(0, slab_rows, GROUP):
            line = index * slab_rows + at
            potential = along_lanes(back_y[line : line + GROUP, :], w_lanes)
            outs[index][at : at + GROUP, :] = potential * (partner_at(places[entry], at) * (1.0 / NG**3))


def exchange_terms(which, slab_rows, places, spectral, partners, weights):
    cells = len(which) * slab_rows * LANES
    vmem = pl.BlockSpec(memory_space=pltpu.VMEM)
    return pl.pallas_call(
        functools.partial(terms_body, which=which),
        out_shape=[jax.ShapeDtypeStruct((slab_rows, LANES), jnp.float32) for _ in which],
        in_specs=[pl.BlockSpec(memory_space=pltpu.SMEM)] + [vmem] * (3 + len(partners)),
        out_specs=[vmem] * len(which),
        scratch_shapes=[pltpu.VMEM((len(which) * slab_rows, LANES), jnp.float32)],
        compiler_params=pltpu.CompilerParams(vmem_limit_bytes=24 << 20),
        cost_estimate=pl.CostEstimate(flops=cells * NG * 12, bytes_accessed=16 * cells, transcendentals=0),
        name="terms",
    )(places, spectral, *partners, weights[1], weights[2])


def blend_body(factors, kept, met, out):
    out[...] = factors[0] * kept[...] + factors[1] * met[...]


def blend(factors, kept, met):
    return kernel_call(blend_body, kept.shape, "svv", 3 * kept.size, 3 * kept.size)(factors, kept, met)


def finish_body(near_sum, arrived, *refs):
    *rows, exchanged, margin = refs
    exchanged[...] = near_sum[...] + arrived[...]
    margin[...] = functools.reduce(jnp.add, [row[...] for row in rows])[:1, : margin.shape[1]]


def finish(near_sum, arrived, rows, columns):
    vmem = pl.BlockSpec(memory_space=pltpu.VMEM)
    return pl.pallas_call(
        finish_body,
        out_shape=[
            jax.ShapeDtypeStruct(near_sum.shape, jnp.float32),
            jax.ShapeDtypeStruct((1, columns), jnp.float32),
        ],
        in_specs=[vmem] * (2 + len(rows)),
        out_specs=[vmem] * 2,
        compiler_params=pltpu.CompilerParams(vmem_limit_bytes=24 << 20),
        cost_estimate=pl.CostEstimate(
            flops=near_sum.size, bytes_accessed=12 * near_sum.size, transcendentals=0
        ),
        name="finish",
    )(near_sum, arrived, *rows)


def seat_body(offsets, places, factors, *, blocks, replicas):
    block, replica = lax.axis_index("blk"), lax.axis_index("rep")
    low, high = replica % 2, replica // 2

    def listed(numbers, index):
        value = jnp.int32(numbers[0])
        for other in range(1, len(numbers)):
            value = jnp.where(index == other, jnp.int32(numbers[other]), value)
        return value

    partners = [block ^ listed(MET, replica), block ^ listed(MET, replica ^ 1)]
    others = [
        block,
        block ^ listed(SENT, replica),
        block ^ listed(SENT, replica ^ 1),
        block ^ listed(SENT, (replica ^ 2) // 2 * 2),
    ]
    far, near = 2 * (1 - high), 2 * high
    same = (listed(MET, replica) == 0).astype(jnp.int32)
    slabs = [far + 1 - low, near + 1 - low, far + low, near + low, low, 2 + low]
    for index, value in enumerate([same, low, high] + slabs + others):
        places[index] = value.astype(jnp.int32)
    shifts = [(offsets[r] + step) % blocks for r in range(replicas) for step in range(STEPS)]
    apart = [(block - partner, 1.0) for partner in partners]
    apart += [(other - partner, 1.0 / NG**3) for partner in partners for other in others]
    for index, (distance, scale) in enumerate(apart):
        wanted = (distance + blocks) % blocks
        hits = jnp.int32(0)
        for shift in shifts:
            hits += (shift == wanted).astype(jnp.int32)
        factors[index] = hits.astype(jnp.float32) * scale


def seat(offsets, blocks, replicas):
    smem = pl.BlockSpec(memory_space=pltpu.SMEM)
    return pl.pallas_call(
        functools.partial(seat_body, blocks=blocks, replicas=replicas),
        out_shape=[
            jax.ShapeDtypeStruct((OTHERS + 4,), jnp.int32),
            jax.ShapeDtypeStruct((10,), jnp.float32),
        ],
        in_specs=[smem],
        out_specs=[smem] * 2,
        name="seat",
    )(offsets)


def gram_body(places, factors, far, met_far, near, met_near, own, *refs):
    *stores, out = refs
    even = places[LOW] == 0
    rows = far.shape[0]
    chunk = 64

    def folded_rows(value):
        return jnp.sum(value.reshape(chunk // 8, 8, LANES), axis=0)

    totals = (jnp.zeros((8, LANES), jnp.float32),) * 8
    for side in range(2):
        is_near = places[HIGH] == side
        piece_a, near_b, moved_a = stores[3 * side : 3 * side + 3]
        own_row = places[OWN + side] * rows

        def step(index, totals, is_near=is_near, piece_a=piece_a, near_b=near_b, moved_a=moved_a, own_row=own_row):
            inside = index * chunk
            at = pl.ds(pl.multiple_of(inside, chunk), chunk)
            mine = pl.ds(pl.multiple_of(own_row + inside, chunk), chunk)
            terms = (
                jnp.where(is_near, near[at, :], far[at, :]),
                jnp.where(is_near, met_near[at, :], met_far[at, :]),
            )
            of_a, of_b = piece_a[at, :], near_b[at, :]
            orbitals = (own[mine, :], jnp.where(even, of_a, of_b), jnp.where(even, of_b, of_a), moved_a[at, :])
            return tuple(
                totals[4 * t + o] + folded_rows(terms[t] * orbitals[o]) for t in range(2) for o in range(4)
            )

        totals = lax.fori_loop(0, rows // chunk, step, totals, unroll=4)
    lane = lax.broadcasted_iota(jnp.int32, (8, LANES), 1)
    result = jnp.zeros((8, LANES), jnp.float32)
    for o in range(4):
        value = jnp.sum(factors[2 + o] * totals[o] + factors[6 + o] * totals[4 + o], axis=(0, 1), keepdims=True)
        result = jnp.where(lane == places[OTHERS + o], value, result)
    out[...] = result


def gram(places, factors, far, near, own, *stores):
    cells = far[0].size
    return kernel_call(
        gram_body, (8, LANES), "ssvvvvv" + "v" * len(stores), 32 * cells, 12 * cells
    )(places, factors, *far, *near, own, *stores)


def position_block(orbital_block, amount):
    bit_count = (lax.axis_size("blk") - 1).bit_length()
    for bit_level in range(bit_count):
        moved_block = passed_along(orbital_block, "blk", 1 << bit_level)
        orbital_block = jnp.where(amount // (1 << bit_level) % 2 == 1, moved_block, orbital_block)
    return orbital_block


def stepped(orbitals, offsets, tables):
    blocks, replicas = lax.axis_size("blk"), lax.axis_size("rep")
    replica = lax.axis_index("rep")
    cells = orbitals.shape[1]
    rows = cells // LANES
    weights = prepared_weights(*tables)
    kernel = screened_kernel(NG)
    first = position_block(orbitals, (offsets[replica] + STEPS // 2) % blocks)
    visits = [first]
    for distance in range(1, STEPS // 2 + 1):
        visits.append(passed_along(first, "blk", -distance))
        visits.append(passed_along(first, "blk", distance))
    own = orbitals.reshape(rows, LANES)
    places = jnp.zeros((OTHERS,), jnp.int32)
    factors = jnp.zeros((2,), jnp.float32)
    whole = jnp.zeros((rows, LANES), jnp.float32)
    for visit in visits:
        visit = visit.reshape(rows, LANES)
        slab_rows = rows // SLABS
        slabs = [visit[slab * slab_rows : (slab + 1) * slab_rows] for slab in range(SLABS)]
        choices = [slabs[index // 2] for index in range(2 * SLABS)]
        head, partner_a = first_planes(0, places, factors, own, choices[:4], weights)
        numbers = jnp.arange(SLABS, dtype=jnp.int32)
        spots = places.at[FAR_SENT : FAR_SENT + SLABS].set(numbers)
        which = tuple(range(FAR_SENT, FAR_SENT + SLABS))
        _, _, *terms = spectrum(
            2, which, spots, factors, own, (head,), (partner_a,), choices[4:], kernel, weights
        )
        whole = whole + jnp.concatenate(terms, axis=0)
    exchanged = lax.psum_scatter(whole.reshape(1, cells), "rep", scatter_dimension=1, tiled=True)
    quarter = lax.dynamic_slice_in_dim(orbitals, replica * (cells // replicas), cells // replicas, 1)
    slab_orbitals = lax.all_to_all(quarter, "blk", split_axis=1, concat_axis=0, tiled=True)
    slab_exchanged = lax.all_to_all(exchanged, "blk", split_axis=1, concat_axis=0, tiled=True)
    partial_value = lax.dot_general(
        slab_orbitals, slab_exchanged, (((1,), (1,)), ((), ())), precision=lax.Precision.HIGHEST
    ) / float(NG**3)
    gram_rows = lax.psum_scatter(partial_value, "blk", scatter_dimension=0, tiled=True)
    return exchanged, lax.psum(gram_rows, "rep")


def folded(orbitals, offsets, tables):
    blocks, replicas = lax.axis_size("blk"), lax.axis_size("rep")
    replica = lax.axis_index("rep")
    cells = orbitals.shape[1]
    rows = cells // LANES
    slab_rows = rows // replicas
    weights = prepared_weights(*tables)
    own = orbitals.reshape(rows, LANES)
    low = replica % 2
    places, factors = seat(offsets, blocks, replicas)

    def along_blocks(value, sent):
        route = [((b ^ sent[r]) * replicas + r, b * replicas + r) for b in range(blocks) for r in range(replicas)]
        return lax.ppermute(value, ("blk", "rep"), route)

    def replica_swap(value, bit):
        return lax.ppermute(value, "rep", [(r, r ^ bit) for r in range(replicas)])

    def slab_of(index):
        return lax.dynamic_slice_in_dim(own, index * slab_rows, slab_rows, 0)

    a_first = along_blocks(slab_of(low), SENT_A)
    b_first = along_blocks(slab_of(1 - low), SENT_B)
    b_last = along_blocks(slab_of(3 - low), SENT_B)
    a_last = along_blocks(slab_of(2 + low), SENT_A)
    kernel = screened_kernel(NG)

    near_a_first = replica_swap(a_first, 1)
    near_b_first = replica_swap(b_first, 1)
    moved_first = replica_swap(a_first, 2)
    head, partner = first_planes(
        0, places, factors, own, (a_first, b_first, near_a_first, near_b_first), weights
    )
    near_a_last = replica_swap(a_last, 1)
    near_b_last = replica_swap(b_last, 1)
    moved_last = replica_swap(a_last, 2)
    third, third_partner = first_planes(2, places, factors, own, (a_last, b_last), weights)
    spectral, last_partner, *sent = spectrum(
        3,
        (FAR_SENT, NEAR_SENT),
        places,
        factors,
        own,
        (head, third),
        (partner, third_partner),
        (near_a_last, near_b_last),
        kernel,
        weights,
    )
    partners = partner, third_partner, last_partner
    met_far = replica_swap(sent[0], 1)
    met_near = replica_swap(sent[1], 1)
    kept = exchange_terms((FAR_KEPT, NEAR_KEPT), slab_rows, places, spectral, partners, weights)
    arrived = replica_swap(blend(factors, kept[0], met_far), 2)
    row = gram(
        places,
        factors,
        (kept[0], met_far),
        (kept[1], met_near),
        own,
        a_first,
        near_b_first,
        moved_first,
        a_last,
        near_b_last,
        moved_last,
    )
    near_sum = blend(factors, kept[1], met_near)
    others = [replica_swap(row, bits) for bits in (2, 3, 1)]
    exchanged, margin = finish(near_sum, arrived, (row, *others), blocks)
    return exchanged.reshape(1, cells // replicas), margin


def local(orbitals, offsets):
    blocks, replicas = lax.axis_size("blk"), lax.axis_size("rep")
    table = cas_table(NG)
    forward = table.reshape(NG, NG // 2, 2).transpose(0, 2, 1).reshape(NG, NG)
    paired = jnp.kron(jnp.eye(2, dtype=jnp.float32), table)
    tables = forward, forward.T, paired
    if is_folded(blocks, replicas):
        return folded(orbitals, offsets, tables)
    return stepped(orbitals, offsets, tables)


def is_folded(blocks, replicas):
    return blocks == replicas == len(MET)


def solution(mesh):
    placed = (P(("groups", "blk"), None), P("groups"))
    step = jax.shard_map(
        local,
        mesh=mesh,
        in_specs=placed,
        out_specs=(P(("groups", "blk"), "rep"), P(("groups", "blk"), None)),
        check_vma=False,
    )
    if not is_folded(mesh.shape["blk"], mesh.shape["rep"]):
        return step
    return step
```

```python
import functools

import jax
import jax.numpy as jnp
from jax import lax
from jax.experimental import pallas as pl
from jax.experimental.pallas import tpu as pltpu
from jax.sharding import PartitionSpec as P


NG = 64
STEPS = 3
LANES = 128
HALF = LANES // 2
PITCH = NG + 1
GROUP = 128
MET = (3, 1, 2, 0)
SENT = (3, 1, 2, 1)
SENT_A = (3, 3, 2, 2)
SENT_B = (1, 1, 1, 1)
SLABS = len(MET)
SAME, LOW, HIGH, FAR_SENT, NEAR_SENT, FAR_KEPT, NEAR_KEPT, OWN, OTHERS = 0, 1, 2, 3, 4, 5, 6, 7, 9
screen_scale = 0.05


def passed_along(block, axis, distance):
    devices = range(lax.axis_size(axis))
    route = [((i - distance) % len(devices), i) for i in devices]
    return lax.ppermute(block, axis, route)


def cas_table(grid_points):
    grid_index = jnp.arange(grid_points, dtype=jnp.int32)
    product = grid_index[:, None] * grid_index[None, :] % grid_points
    phase_angle = 2.0 * jnp.pi / grid_points * product.astype(jnp.float32)
    return jnp.cos(phase_angle) + jnp.sin(phase_angle)


def screened_kernel(grid_points):
    def squares(index):
        folded = jnp.where(index <= grid_points // 2, index, index - grid_points).astype(jnp.float32)
        return folded * folded

    shape = (grid_points * grid_points // 2, 2 * grid_points)
    row = lax.broadcasted_iota(jnp.int32, shape, 0)
    lane = lax.broadcasted_iota(jnp.int32, shape, 1)
    k_squared = (
        squares(row % grid_points)
        + squares(2 * (row // grid_points) + lane // grid_points)
        + squares(lane % grid_points)
    )
    safe_square = jnp.maximum(k_squared, 1.0)
    screened = (
        4.0
        * jnp.pi
        / (screen_scale * safe_square)
        * (1.0 - jnp.exp(-screen_scale * safe_square / (4.0 * jnp.pi)))
    )
    return jnp.where(k_squared > 0.5, screened, jnp.ones_like(screened))


def high_low(value):
    high = value.astype(jnp.bfloat16)
    return high, (value - high.astype(jnp.float32)).astype(jnp.bfloat16)


def dot(a, b):
    return lax.dot_general(a, b, (((1,), (0,)), ((), ())), preferred_element_type=jnp.float32)


def swapped(first, second, low_half):
    return (
        jnp.where(low_half, first, pltpu.roll(second, HALF, 1)),
        jnp.where(low_half, pltpu.roll(first, HALF, 1), second),
    )


def left_weights(table):
    high, low = high_low(table)
    return jnp.concatenate([high, high, low], axis=1)


def lane_weights(table):
    high, low = high_low(table)
    return jnp.concatenate(
        [jnp.concatenate([high, low], axis=1), jnp.concatenate([high, jnp.zeros_like(low)], axis=1)],
        axis=0,
    )


def from_left(weights, value):
    high, low = high_low(value)
    return dot(weights, jnp.concatenate([high, low, high], axis=0))


def along_lanes(value, weights):
    high, low = high_low(value)
    both = dot(jnp.concatenate([high, low], axis=1), weights)
    return both[:, :LANES] + both[:, LANES:]


def low_mask(rows):
    return lax.broadcasted_iota(jnp.int32, (rows, LANES), 1) < HALF


def kernel_call(body, shape, spaces, flops, cells, **more):
    memory = {"s": pltpu.SMEM, "v": pltpu.VMEM}
    return pl.pallas_call(
        body,
        out_shape=jax.ShapeDtypeStruct(shape, jnp.float32),
        in_specs=[pl.BlockSpec(memory_space=memory[space]) for space in spaces],
        out_specs=pl.BlockSpec(memory_space=pltpu.VMEM),
        compiler_params=pltpu.CompilerParams(vmem_limit_bytes=24 << 20),
        cost_estimate=pl.CostEstimate(flops=flops, bytes_accessed=4 * cells, transcendentals=0),
        **more,
    )


def weights_body(forward, backward, paired, left_y, left_back, lanes):
    left_y[...] = left_weights(forward[...])
    left_back[...] = left_weights(backward[...])
    lanes[...] = lane_weights(paired[...])


def prepared_weights(forward, backward, paired):
    vmem = pl.BlockSpec(memory_space=pltpu.VMEM)
    shapes = (NG, 3 * NG), (NG, 3 * NG), (2 * LANES, 2 * LANES)
    return pl.pallas_call(
        weights_body,
        out_shape=[jax.ShapeDtypeStruct(shape, jnp.bfloat16) for shape in shapes],
        in_specs=[vmem] * 3,
        out_specs=[vmem] * 3,
        name="weights",
    )(forward, backward, paired)


def planes_body(own, visit_at, alone, left_y, lanes, along_z, out, *, first_row):
    plane = NG // 2
    mask = low_mask(plane)
    w_forward = left_y[...]
    w_lanes = lanes[...]
    rows = along_z.shape[0]
    for at in range(0, rows, GROUP):
        mine = own[first_row + at : first_row + at + GROUP, :]
        density = mine * jnp.where(alone, mine, visit_at(at))
        along_z[at : at + GROUP, :] = along_lanes(density, w_lanes)

    def step_planes(step, _):
        at = step * (4 * plane)
        blocks = []
        for half in range(2):
            base = at + half * 2 * plane
            lines = [along_z[pl.ds(pl.multiple_of(base + odd * plane, plane), plane), :] for odd in range(2)]
            blocks.append(jnp.concatenate(swapped(*lines, mask), axis=0))
        along_y = from_left(w_forward, jnp.concatenate(blocks, axis=1))
        out[pl.ds(step * (2 * PITCH), NG), :] = along_y[:, :LANES]
        out[pl.ds(step * (2 * PITCH) + PITCH, NG), :] = along_y[:, LANES:]
        return 0

    steps = rows // (4 * plane)
    lax.fori_loop(0, steps, step_planes, 0, unroll=steps)


def slabs_body(places, own, choices, left_y, lanes, along_z, out, partner, *, first_slab):
    slab_rows = choices[0].shape[0]
    even = places[LOW] == 0
    alone = places[SAME] == 1
    first_row = first_slab * slab_rows

    def visit_at(at):
        inside = slice(at % slab_rows, at % slab_rows + GROUP)
        index = at // slab_rows * 2
        value = jnp.where(even, choices[index][inside, :], choices[index + 1][inside, :])
        partner[at : at + GROUP, :] = jnp.where(alone, own[first_row + at : first_row + at + GROUP, :], value)
        return value

    planes_body(own, visit_at, alone, left_y, lanes, along_z, out, first_row=first_row)


def first_body(places, factors, own, *refs, first_slab, count):
    choices, (left_y, lanes, out, partner, along_z) = refs[: 2 * count], refs[2 * count :]
    slabs_body(places, own, choices, left_y, lanes, along_z, out, partner, first_slab=first_slab)


def spectrum_body(places, factors, own, *refs, heads, first_slab, count, which):
    parts, known, rest = refs[:heads], refs[heads : 2 * heads], refs[2 * heads :]
    choices, rest = rest[: 2 * count], rest[2 * count :]
    kernel, left_y, left_back, lanes, out, partner, *outs, tail, along_z, back_y = rest
    plane = NG // 2
    mask = low_mask(plane)
    slabs_body(places, own, choices, left_y, lanes, along_z, tail, partner, first_slab=first_slab)
    parts = (*parts, tail)
    w_forward = left_y[...]
    w_backward = left_back[...]

    def columns(step, _):
        blocks = []
        for part in range(2):
            row = 4 * step + 2 * part
            first, second = (
                jnp.concatenate(
                    [ref[pl.ds(row + odd, ref.shape[0] // PITCH, stride=PITCH), :] for ref in parts], axis=0
                )
                for odd in range(2)
            )
            blocks.append(jnp.concatenate(swapped(first, second, mask), axis=0))
        along_x = from_left(w_forward, jnp.concatenate(blocks, axis=1))
        at = pl.multiple_of(step * (2 * NG), 2 * NG)
        weight = jnp.concatenate([kernel[pl.ds(at, NG), :], kernel[pl.ds(at + NG, NG), :]], axis=1)
        returned = from_left(w_backward, along_x * weight)
        for part in range(2):
            block = returned[:, part * LANES : (part + 1) * LANES]
            row = 4 * step + 2 * part
            for odd, value in enumerate(swapped(block[:plane], block[plane:], mask)):
                out[pl.ds(row + odd, plane, stride=PITCH), :] = value
        return 0

    lax.fori_loop(0, NG // 4, columns, 0, unroll=NG // 4)
    fill_terms(places, out, (*known, partner), left_back, lanes, outs, back_y, which)


def planes_call(body, spaces, out_rows, scratch_rows, flops, cells):
    smem = pl.BlockSpec(memory_space=pltpu.SMEM)
    vmem = pl.BlockSpec(memory_space=pltpu.VMEM)
    return pl.pallas_call(
        body,
        out_shape=[jax.ShapeDtypeStruct((rows, LANES), jnp.float32) for rows in out_rows],
        in_specs=[smem] * 2 + [vmem] * spaces,
        out_specs=[vmem] * len(out_rows),
        scratch_shapes=[pltpu.VMEM((rows, LANES), jnp.float32) for rows in scratch_rows],
        compiler_params=pltpu.CompilerParams(vmem_limit_bytes=24 << 20),
        cost_estimate=pl.CostEstimate(flops=flops, bytes_accessed=4 * cells, transcendentals=0),
    )


def first_planes(first_slab, places, factors, own, choices, weights):
    left_y, _, lanes = weights
    count = len(choices) // 2
    rows = count * choices[0].shape[0]
    body = functools.partial(first_body, first_slab=first_slab, count=count)
    pitched = rows // NG * PITCH
    return planes_call(
        body, 3 + 2 * count, (pitched, rows), (rows,), rows * LANES * NG * 4, 4 * rows * LANES
    )(places, factors, own, *choices, left_y, lanes)


def spectrum(first_slab, which, places, factors, own, heads, known, choices, kernel, weights):
    count = len(choices) // 2
    rows, slab_rows = own.shape[0], choices[0].shape[0]
    last = count * slab_rows
    body = functools.partial(spectrum_body, heads=len(heads), first_slab=first_slab, count=count, which=which)
    return planes_call(
        body,
        5 + 2 * len(heads) + 2 * count,
        (rows // NG * PITCH, last) + (slab_rows,) * len(which),
        (last // NG * PITCH, last, len(which) * slab_rows),
        rows * LANES * NG * 16,
        8 * rows * LANES,
    )(places, factors, own, *heads, *known, *choices, kernel, *weights)


def terms_body(places, spectral, *refs, which):
    partners, (left_back, lanes, *outs, back_y) = refs[: -3 - len(which)], refs[-3 - len(which) :]
    fill_terms(places, spectral, partners, left_back, lanes, outs, back_y, which)


def fill_terms(places, spectral, partners, left_back, lanes, outs, back_y, which):
    plane = NG // 2
    mask = low_mask(plane)
    w_backward = left_back[...]
    w_lanes = lanes[...]
    slab_rows = outs[0].shape[0]
    steps = slab_rows // (4 * plane)

    def partner_at(slab, at):
        value, first_slab = None, 0
        for piece in partners:
            count = piece.shape[0] // slab_rows
            row = jnp.clip(slab - first_slab, 0, count - 1) * slab_rows + at
            here = piece[pl.ds(pl.multiple_of(row, 8), GROUP), :]
            value = here if value is None else jnp.where(slab >= first_slab, here, value)
            first_slab += count
        return value

    for index, entry in enumerate(which):
        start = places[entry] * slab_rows
        for step in range(steps):
            row = (start // NG + 2 * step) * PITCH
            pair = jnp.concatenate([spectral[pl.ds(row, NG), :], spectral[pl.ds(row + PITCH, NG), :]], axis=1)
            along_y = from_left(w_backward, pair)
            for half in range(2):
                block = along_y[:, half * LANES : (half + 1) * LANES]
                for second, value in enumerate(swapped(block[:plane], block[plane:], mask)):
                    line = index * slab_rows + (4 * step + 2 * half + second) * plane
                    back_y[line : line + plane, :] = value
    for index, entry in enumerate(which):
        for at in range(0, slab_rows, GROUP):
            line = index * slab_rows + at
            potential = along_lanes(back_y[line : line + GROUP, :], w_lanes)
            outs[index][at : at + GROUP, :] = potential * (partner_at(places[entry], at) * (1.0 / NG**3))


def exchange_terms(which, slab_rows, places, spectral, partners, weights):
    cells = len(which) * slab_rows * LANES
    vmem = pl.BlockSpec(memory_space=pltpu.VMEM)
    return pl.pallas_call(
        functools.partial(terms_body, which=which),
        out_shape=[jax.ShapeDtypeStruct((slab_rows, LANES), jnp.float32) for _ in which],
        in_specs=[pl.BlockSpec(memory_space=pltpu.SMEM)] + [vmem] * (3 + len(partners)),
        out_specs=[vmem] * len(which),
        scratch_shapes=[pltpu.VMEM((len(which) * slab_rows, LANES), jnp.float32)],
        compiler_params=pltpu.CompilerParams(vmem_limit_bytes=24 << 20),
        cost_estimate=pl.CostEstimate(flops=cells * NG * 12, bytes_accessed=16 * cells, transcendentals=0),
        name="terms",
    )(places, spectral, *partners, weights[1], weights[2])


def blend_body(factors, kept, met, out):
    out[...] = factors[0] * kept[...] + factors[1] * met[...]


def blend(factors, kept, met):
    return kernel_call(blend_body, kept.shape, "svv", 3 * kept.size, 3 * kept.size)(factors, kept, met)


def finish_body(near_sum, arrived, *refs):
    *rows, exchanged, margin = refs
    exchanged[...] = near_sum[...] + arrived[...]
    margin[...] = functools.reduce(jnp.add, [row[...] for row in rows])[:1, : margin.shape[1]]


def finish(near_sum, arrived, rows, columns):
    vmem = pl.BlockSpec(memory_space=pltpu.VMEM)
    return pl.pallas_call(
        finish_body,
        out_shape=[
            jax.ShapeDtypeStruct(near_sum.shape, jnp.float32),
            jax.ShapeDtypeStruct((1, columns), jnp.float32),
        ],
        in_specs=[vmem] * (2 + len(rows)),
        out_specs=[vmem] * 2,
        compiler_params=pltpu.CompilerParams(vmem_limit_bytes=24 << 20),
        cost_estimate=pl.CostEstimate(
            flops=near_sum.size, bytes_accessed=12 * near_sum.size, transcendentals=0
        ),
        name="finish",
    )(near_sum, arrived, *rows)


def seat_body(offsets, places, factors, *, blocks, replicas):
    block, replica = lax.axis_index("blk"), lax.axis_index("rep")
    low, high = replica % 2, replica // 2

    def listed(numbers, index):
        value = jnp.int32(numbers[0])
        for other in range(1, len(numbers)):
            value = jnp.where(index == other, jnp.int32(numbers[other]), value)
        return value

    partners = [block ^ listed(MET, replica), block ^ listed(MET, replica ^ 1)]
    others = [
        block,
        block ^ listed(SENT, replica),
        block ^ listed(SENT, replica ^ 1),
        block ^ listed(SENT, (replica ^ 2) // 2 * 2),
    ]
    far, near = 2 * (1 - high), 2 * high
    same = (listed(MET, replica) == 0).astype(jnp.int32)
    slabs = [far + 1 - low, near + 1 - low, far + low, near + low, low, 2 + low]
    for index, value in enumerate([same, low, high] + slabs + others):
        places[index] = value.astype(jnp.int32)
    shifts = [(offsets[r] + step) % blocks for r in range(replicas) for step in range(STEPS)]
    apart = [(block - partner, 1.0) for partner in partners]
    apart += [(other - partner, 1.0 / NG**3) for partner in partners for other in others]
    for index, (distance, scale) in enumerate(apart):
        wanted = (distance + blocks) % blocks
        hits = jnp.int32(0)
        for shift in shifts:
            hits += (shift == wanted).astype(jnp.int32)
        factors[index] = hits.astype(jnp.float32) * scale


def seat(offsets, blocks, replicas):
    smem = pl.BlockSpec(memory_space=pltpu.SMEM)
    return pl.pallas_call(
        functools.partial(seat_body, blocks=blocks, replicas=replicas),
        out_shape=[
            jax.ShapeDtypeStruct((OTHERS + 4,), jnp.int32),
            jax.ShapeDtypeStruct((10,), jnp.float32),
        ],
        in_specs=[smem],
        out_specs=[smem] * 2,
        name="seat",
    )(offsets)


def gram_body(places, factors, far, met_far, near, met_near, own, *refs):
    *stores, out = refs
    even = places[LOW] == 0
    rows = far.shape[0]
    chunk = 32

    def folded_rows(value):
        return jnp.sum(value.reshape(chunk // 8, 8, LANES), axis=0)

    totals = (jnp.zeros((8, LANES), jnp.float32),) * 8
    for side in range(2):
        is_near = places[HIGH] == side
        piece_a, near_b, moved_a = stores[3 * side : 3 * side + 3]
        own_row = places[OWN + side] * rows

        def step(index, totals, is_near=is_near, piece_a=piece_a, near_b=near_b, moved_a=moved_a, own_row=own_row):
            inside = index * chunk
            at = pl.ds(pl.multiple_of(inside, chunk), chunk)
            mine = pl.ds(pl.multiple_of(own_row + inside, chunk), chunk)
            terms = (
                jnp.where(is_near, near[at, :], far[at, :]),
                jnp.where(is_near, met_near[at, :], met_far[at, :]),
            )
            of_a, of_b = piece_a[at, :], near_b[at, :]
            orbitals = (own[mine, :], jnp.where(even, of_a, of_b), jnp.where(even, of_b, of_a), moved_a[at, :])
            return tuple(
                totals[4 * t + o] + folded_rows(terms[t] * orbitals[o]) for t in range(2) for o in range(4)
            )

        totals = lax.fori_loop(0, rows // chunk, step, totals, unroll=8)
    lane = lax.broadcasted_iota(jnp.int32, (8, LANES), 1)
    result = jnp.zeros((8, LANES), jnp.float32)
    for o in range(4):
        value = jnp.sum(factors[2 + o] * totals[o] + factors[6 + o] * totals[4 + o], axis=(0, 1), keepdims=True)
        result = jnp.where(lane == places[OTHERS + o], value, result)
    out[...] = result


def gram(places, factors, far, near, own, *stores):
    cells = far[0].size
    return kernel_call(
        gram_body, (8, LANES), "ssvvvvv" + "v" * len(stores), 32 * cells, 12 * cells
    )(places, factors, *far, *near, own, *stores)


def position_block(orbital_block, amount):
    bit_count = (lax.axis_size("blk") - 1).bit_length()
    for bit_level in range(bit_count):
        moved_block = passed_along(orbital_block, "blk", 1 << bit_level)
        orbital_block = jnp.where(amount // (1 << bit_level) % 2 == 1, moved_block, orbital_block)
    return orbital_block


def stepped(orbitals, offsets, tables):
    blocks, replicas = lax.axis_size("blk"), lax.axis_size("rep")
    replica = lax.axis_index("rep")
    cells = orbitals.shape[1]
    rows = cells // LANES
    weights = prepared_weights(*tables)
    kernel = screened_kernel(NG)
    first = position_block(orbitals, (offsets[replica] + STEPS // 2) % blocks)
    visits = [first]
    for distance in range(1, STEPS // 2 + 1):
        visits.append(passed_along(first, "blk", -distance))
        visits.append(passed_along(first, "blk", distance))
    own = orbitals.reshape(rows, LANES)
    places = jnp.zeros((OTHERS,), jnp.int32)
    factors = jnp.zeros((2,), jnp.float32)
    whole = jnp.zeros((rows, LANES), jnp.float32)
    for visit in visits:
        visit = visit.reshape(rows, LANES)
        slab_rows = rows // SLABS
        slabs = [visit[slab * slab_rows : (slab + 1) * slab_rows] for slab in range(SLABS)]
        choices = [slabs[index // 2] for index in range(2 * SLABS)]
        head, partner_a = first_planes(0, places, factors, own, choices[:4], weights)
        numbers = jnp.arange(SLABS, dtype=jnp.int32)
        spots = places.at[FAR_SENT : FAR_SENT + SLABS].set(numbers)
        which = tuple(range(FAR_SENT, FAR_SENT + SLABS))
        _, _, *terms = spectrum(
            2, which, spots, factors, own, (head,), (partner_a,), choices[4:], kernel, weights
        )
        whole = whole + jnp.concatenate(terms, axis=0)
    exchanged = lax.psum_scatter(whole.reshape(1, cells), "rep", scatter_dimension=1, tiled=True)
    quarter = lax.dynamic_slice_in_dim(orbitals, replica * (cells // replicas), cells // replicas, 1)
    slab_orbitals = lax.all_to_all(quarter, "blk", split_axis=1, concat_axis=0, tiled=True)
    slab_exchanged = lax.all_to_all(exchanged, "blk", split_axis=1, concat_axis=0, tiled=True)
    partial_value = lax.dot_general(
        slab_orbitals, slab_exchanged, (((1,), (1,)), ((), ())), precision=lax.Precision.HIGHEST
    ) / float(NG**3)
    gram_rows = lax.psum_scatter(partial_value, "blk", scatter_dimension=0, tiled=True)
    return exchanged, lax.psum(gram_rows, "rep")


def folded(orbitals, offsets, tables):
    blocks, replicas = lax.axis_size("blk"), lax.axis_size("rep")
    replica = lax.axis_index("rep")
    cells = orbitals.shape[1]
    rows = cells // LANES
    slab_rows = rows // replicas
    weights = prepared_weights(*tables)
    own = orbitals.reshape(rows, LANES)
    low = replica % 2
    places, factors = seat(offsets, blocks, replicas)

    def along_blocks(value, sent):
        route = [((b ^ sent[r]) * replicas + r, b * replicas + r) for b in range(blocks) for r in range(replicas)]
        return lax.ppermute(value, ("blk", "rep"), route)

    def replica_swap(value, bit):
        return lax.ppermute(value, "rep", [(r, r ^ bit) for r in range(replicas)])

    def slab_of(index):
        return lax.dynamic_slice_in_dim(own, index * slab_rows, slab_rows, 0)

    a_first = along_blocks(slab_of(low), SENT_A)
    b_first = along_blocks(slab_of(1 - low), SENT_B)
    b_last = along_blocks(slab_of(3 - low), SENT_B)
    a_last = along_blocks(slab_of(2 + low), SENT_A)
    kernel = screened_kernel(NG)

    near_a_first = replica_swap(a_first, 1)
    near_b_first = replica_swap(b_first, 1)
    moved_first = replica_swap(a_first, 2)
    head, partner = first_planes(
        0, places, factors, own, (a_first, b_first, near_a_first, near_b_first), weights
    )
    near_a_last = replica_swap(a_last, 1)
    near_b_last = replica_swap(b_last, 1)
    moved_last = replica_swap(a_last, 2)
    third, third_partner = first_planes(2, places, factors, own, (a_last, b_last), weights)
    spectral, last_partner, *sent = spectrum(
        3,
        (FAR_SENT, NEAR_SENT),
        places,
        factors,
        own,
        (head, third),
        (partner, third_partner),
        (near_a_last, near_b_last),
        kernel,
        weights,
    )
    partners = partner, third_partner, last_partner
    met_far = replica_swap(sent[0], 1)
    met_near = replica_swap(sent[1], 1)
    kept = exchange_terms((FAR_KEPT, NEAR_KEPT), slab_rows, places, spectral, partners, weights)
    arrived = replica_swap(blend(factors, kept[0], met_far), 2)
    row = gram(
        places,
        factors,
        (kept[0], met_far),
        (kept[1], met_near),
        own,
        a_first,
        near_b_first,
        moved_first,
        a_last,
        near_b_last,
        moved_last,
    )
    near_sum = blend(factors, kept[1], met_near)
    others = [replica_swap(row, bits) for bits in (2, 3, 1)]
    exchanged, margin = finish(near_sum, arrived, (row, *others), blocks)
    return exchanged.reshape(1, cells // replicas), margin


def local(orbitals, offsets):
    blocks, replicas = lax.axis_size("blk"), lax.axis_size("rep")
    table = cas_table(NG)
    forward = table.reshape(NG, NG // 2, 2).transpose(0, 2, 1).reshape(NG, NG)
    paired = jnp.kron(jnp.eye(2, dtype=jnp.float32), table)
    tables = forward, forward.T, paired
    if is_folded(blocks, replicas):
        return folded(orbitals, offsets, tables)
    return stepped(orbitals, offsets, tables)


def is_folded(blocks, replicas):
    return blocks == replicas == len(MET)


def solution(mesh):
    placed = (P(("groups", "blk"), None), P("groups"))
    step = jax.shard_map(
        local,
        mesh=mesh,
        in_specs=placed,
        out_specs=(P(("groups", "blk"), "rep"), P(("groups", "blk"), None)),
        check_vma=False,
    )
    if not is_folded(mesh.shape["blk"], mesh.shape["rep"]):
        return step
    return step
```
